128 devices in a mesh: hist: 8 (over x, core), tsec: 16 (over z, y).
Axes of the slice: x: 4, y: 4, z: 4, core: 2. Of those that a mesh axis runs over, the one named last changes fastest.
Arguments:
- hist_green: bfloat16 [2, 16384, 16384], P(None, 'hist', 'tsec'), may hold values from -6 to 6
- sigma_panel: bfloat16 [16384, 512], P('hist'), may hold values from -0.03125 to 0.03125
- step_operator: float32 [2, 2, 256, 256], replicated, as said below
- coupling: float32 [8, 1024], replicated, may hold values from -0.01953125 to 0.01953125
- pair_index: int32 [3, 8, 1024], replicated, may hold values from 0 to 1023
Outputs:
- new_rows: float32 [2, 16, 1024, 512], P(None, 'tsec', 'hist')
- new_sigma: bfloat16 [2, 16, 1024, 512], P(None, 'tsec', 'hist')
The draws below stay inside these ranges and needn't reach their ends.
Inputs may be any that keep to these rules, and one draw needn't show every extreme that they name: `step_operator`: for each block the real part is symmetric and the imaginary part antisymmetric; the diagonal of the real part exceeds the sum of magnitudes of the rest of its row in the real form, so the operator is Hermitian positive definite.
All inputs are finite; a program needn't handle non-finite values.
Results may differ from the reference program's by a relative error of at most 0.0058.
Values may be sent and summed in bfloat16 or wider, within the bound.
A program may use at most 128 MiB of HBM per device.

```python
import jax
import jax.numpy as jnp
from jax import lax

N = 32
B = 8
NBLK = 2
Q = 8
SEC_DEV = 32
PAST = 512
TBLOCKS = 16


def draw_step_operator(key, part):
    order_size = B * N
    key_off = jax.random.fold_in(key, 11)
    key_diag = jax.random.fold_in(key, 23)
    raw_values = jax.random.uniform(key_off, (NBLK, 2, order_size, order_size), jnp.float32, -1.0, 1.0) * 0.0028
    real_part = 0.5 * (raw_values[:, 0] + jnp.swapaxes(raw_values[:, 0], 1, 2))
    imag_part = 0.5 * (raw_values[:, 1] - jnp.swapaxes(raw_values[:, 1], 1, 2))
    diag_values = jax.random.uniform(key_diag, (NBLK, order_size), jnp.float32, 1.5, 3.0)
    real_part = real_part + diag_values[:, :, None] * jnp.eye(order_size, dtype=jnp.float32)
    return jnp.stack([real_part, imag_part], axis=1)


def plant(result, stream_key, low, high):
    longest = result.shape.index(max(result.shape))
    spots = []
    for shift in (0, 1):
        where = [jax.random.randint(jax.random.fold_in(stream_key, axis), (), 0, length) for axis, length in enumerate(result.shape)]
        where[longest] = (where[longest] + shift) % result.shape[longest]
        spots.append(tuple(where))
    return result.at[spots[0]].set(low).at[spots[1]].set(high)


def levels(key, shape, pieces, least, high):
    loudness, own = 1.0, jax.random.fold_in(key, 6)
    for position, parts in pieces:
        draws = jnp.exp(jax.random.uniform(jax.random.fold_in(own, position), (parts,), jnp.float32, least / len(pieces), high / len(pieces)))
        loudness = loudness * jnp.repeat(draws, shape[position] // parts).reshape([-1 if axis == position else 1 for axis in range(len(shape))])
    return loudness


def gaussian(stream_key, shape, width, limit, shards=(), held_as=jnp.bfloat16):
    result = jax.random.normal(stream_key, shape, jnp.float32) * width
    if len(shards) > 0:
        result = levels(stream_key, shape, shards, -0.22, 0.18) * result
    return jnp.clip(result, min=-limit, max=limit).astype(held_as)


def setup_inputs(seed: int = 0) -> dict:
    streams_of = jax.random.split(jax.random.key(seed), 6)
    hist_green = gaussian(streams_of[0], (2, PAST * N, PAST * N), 1.0, 6.0, ((1, 8), (2, 16)))
    sigma_panel = gaussian(streams_of[1], (PAST * N, 2 * B * N), (2 * PAST * N) ** -0.5, 0.03125, ((0, 8),))
    step_operator = draw_step_operator(jax.random.fold_in(streams_of[5], 71), 0)
    coupling = gaussian(streams_of[3], (Q, N * N), (6 * PAST * N) ** -0.5, 0.01953125, (), jnp.float32)
    pair_index = plant(jax.random.randint(streams_of[4], (3, Q, N * N), 0, N * N), jax.random.fold_in(streams_of[4], 1), 0, (N * N) - 1).astype(jnp.int32)
    return dict(hist_green=hist_green, sigma_panel=sigma_panel, step_operator=step_operator, coupling=coupling, pair_index=pair_index)


def turned_panel(panel, half_width):
    return jnp.concatenate([-panel[:, half_width:], panel[:, :half_width]], axis=1)

def memory_full(hist_green, panel, half_width):
    column_total = hist_green.shape[2]
    span_width = SEC_DEV * N
    turned = turned_panel(panel, half_width)
    starts = jnp.arange(column_total // span_width, dtype=jnp.int32) * span_width

    def one_block(col_start):
        green_real = lax.dynamic_slice_in_dim(hist_green[0], col_start, span_width, 1)
        green_imag = lax.dynamic_slice_in_dim(hist_green[1], col_start, span_width, 1)
        first_term = jnp.dot(green_real.T.astype(jnp.float32), panel.astype(jnp.float32), preferred_element_type=jnp.float32)
        return first_term + jnp.dot(green_imag.T.astype(jnp.float32), turned.astype(jnp.float32), preferred_element_type=jnp.float32)
    return lax.map(one_block, starts).reshape(column_total, 2 * half_width)

def block_solve(operator, rhs_rows):
    real_part = operator[0]
    imag_part = operator[1]
    upper_half = jnp.concatenate([real_part, -imag_part], axis=1)
    lower_half = jnp.concatenate([imag_part, real_part], axis=1)
    factor = jnp.linalg.cholesky(jnp.concatenate([upper_half, lower_half], axis=0))
    return jax.scipy.linalg.cho_solve((factor, True), rhs_rows.T).T

def self_energy(row_block, pair_index, coupling, orbit, times):
    slots = row_block.shape[0] // orbit
    field = row_block.reshape(slots, orbit, 2, times, orbit).transpose(4, 1, 2, 3, 0)
    field = field.reshape(orbit * orbit, 2, times * slots)
    term_count = pair_index.shape[1]

    def select_pairs(which):
        taken = jnp.take(field, pair_index[which].reshape(-1), axis=0)
        return taken.reshape(term_count, orbit * orbit, 2, times * slots)
    first_term = select_pairs(0)
    second_term = select_pairs(1)
    third_term = select_pairs(2)
    prod_real = first_term[:, :, 0] * second_term[:, :, 0] - first_term[:, :, 1] * second_term[:, :, 1]
    prod_imag = first_term[:, :, 0] * second_term[:, :, 1] + first_term[:, :, 1] * second_term[:, :, 0]
    trip_real = prod_real * third_term[:, :, 0] + prod_imag * third_term[:, :, 1]
    trip_imag = prod_imag * third_term[:, :, 0] - prod_real * third_term[:, :, 1]
    weights = coupling[:, :, None]
    sig_real = jnp.sum(trip_real * weights, axis=0)
    sig_imag = jnp.sum(trip_imag * weights, axis=0)
    stacked = jnp.stack([sig_real, sig_imag], axis=1).reshape(orbit, orbit, 2, times, slots)
    stacked = stacked.transpose(4, 1, 2, 3, 0).reshape(slots * orbit, 2 * times * orbit)
    return stacked.astype(jnp.bfloat16)

def reference(hist_green, sigma_panel, step_operator, coupling, pair_index):
    half_width = B * N
    column_total = hist_green.shape[2]
    tail_rows = hist_green[:, hist_green.shape[1] - half_width:, :]
    previous = tail_rows.astype(jnp.float32).transpose(2, 0, 1).reshape(column_total, 2 * half_width)
    panel = sigma_panel
    solved_list = []
    sigma_list = []
    for block_index in range(NBLK):
        memory = memory_full(hist_green, panel, half_width)
        solution = block_solve(step_operator[block_index], previous + memory)
        sigma_new = self_energy(solution, pair_index, coupling, N, B)
        solved_list.append(solution.reshape(TBLOCKS, SEC_DEV * N, 2 * half_width))
        sigma_list.append(sigma_new.reshape(TBLOCKS, SEC_DEV * N, 2 * half_width))
        previous = solution
        panel = sigma_new
    return (jnp.stack(solved_list), jnp.stack(sigma_list))
```

```python
import functools

import jax
import jax.numpy as jnp
from jax import lax
from jax.experimental import pallas as pl
from jax.experimental.pallas import tpu as pltpu
from jax.sharding import PartitionSpec as P

N = 32
B = 8
NBLK = 2
Q = 8
HALF = B * N
WIDE = 2 * HALF
LANES = 128
PAIRS = N * N
TILES = PAIRS // LANES
MESH = pl.DeviceIdType.MESH
f32, bf16, i32 = jnp.float32, jnp.bfloat16, jnp.int32
HIGHEST = lax.Precision.HIGHEST
PEAK = 32000.0


def dot(left, right, precision=None):
    return jnp.dot(left, right, preferred_element_type=f32, precision=precision)


def inverse_kernel(op_ref, out_ref, a_ref, x_ref, r_ref):
    block = pl.program_id(0)
    rows = lax.broadcasted_iota(i32, (HALF, HALF), 0)
    cols = lax.broadcasted_iota(i32, (HALF, HALF), 1)
    eye = jnp.where(rows == cols, 1.0, 0.0).astype(f32)
    real, imag = op_ref[block, 0], op_ref[block, 1]
    a_ref[0], a_ref[1] = real, imag
    inv_row = 1.0 / jnp.sum(real * eye, axis=0, keepdims=True)
    r_ref[0] = eye - real * inv_row
    r_ref[1] = -imag * inv_row
    x_ref[0] = eye * inv_row
    x_ref[1] = jnp.zeros((HALF, HALF), f32)

    def worst():
        return jnp.max(jnp.maximum(jnp.abs(r_ref[0]), jnp.abs(r_ref[1])))

    def unfinished(carry):
        step, size = carry
        return jnp.logical_and(step < 40, size > 1e-6)

    def improve(carry):
        step, _ = carry
        xr, xi, rr, ri = x_ref[0], x_ref[1], r_ref[0], r_ref[1]
        x_ref[0] = xr + (dot(xr, rr, HIGHEST) - dot(xi, ri, HIGHEST))
        x_ref[1] = xi + (dot(xr, ri, HIGHEST) + dot(xi, rr, HIGHEST))
        xr, xi, ar, ai = x_ref[0], x_ref[1], a_ref[0], a_ref[1]
        r_ref[0] = eye - (dot(ar, xr, HIGHEST) - dot(ai, xi, HIGHEST))
        r_ref[1] = -(dot(ar, xi, HIGHEST) + dot(ai, xr, HIGHEST))
        return step + 1, worst()

    lax.while_loop(unfinished, improve, (jnp.int32(0), worst()))
    xr, xi = x_ref[0], x_ref[1]
    out_ref[0, :HALF, :HALF] = xr
    out_ref[0, :HALF, HALF:] = -xi
    out_ref[0, HALF:, :HALF] = xi
    out_ref[0, HALF:, HALF:] = xr


def invert(step_operator):
    return pl.pallas_call(
        inverse_kernel,
        grid=(NBLK,),
        out_shape=jax.ShapeDtypeStruct((NBLK, WIDE, WIDE), f32),
        in_specs=[pl.BlockSpec(memory_space=pltpu.VMEM)],
        out_specs=pl.BlockSpec((1, WIDE, WIDE), lambda k: (k, 0, 0)),
        scratch_shapes=[pltpu.VMEM((2, HALF, HALF), f32)] * 3,
        compiler_params=pltpu.CompilerParams(vmem_limit_bytes=32 << 20),
    )(step_operator)


def window_kernel(
    green_hbm, panel_ref, inv_ref, pair_ref, weight_ref,
    rows_ref, sigma_ref,
    green, panel_next, held, field, packed, spread, sig, sigma_out,
    sib_send, sib_recv, sums, hop_recv, end_recv,
    load_sem, sib_ss, sib_rs, hop_ss, hop_rs, end_ss, end_rs, gat_ss, gat_rs, gat_ls,
):
    hist, tsec = lax.axis_index("hist"), lax.axis_index("tsec")
    chip, core = hist // 2, hist % 2
    right = ((chip + 1) % 4) * 2 + core
    left = ((chip + 3) % 4) * 2 + core
    sibling = chip * 2 + 1 - core
    target = tsec // 2

    def loads(d):
        lanes = pl.ds(pl.multiple_of(d * LANES, LANES), LANES)
        return [
            pltpu.make_async_copy(
                green_hbm.at[part, :, lanes],
                green.at[d, :, pl.ds(part * LANES, LANES)],
                load_sem.at[d, part],
            )
            for part in range(2)
        ]

    for o in (2, 1, 3, 0):
        for d in (((chip + o) % 4) * 2 + 1 - core, ((chip + o) % 4) * 2 + core):
            for copy in loads(d):
                copy.start()

    barrier = pltpu.get_barrier_semaphore()
    for h in (right, left, sibling):
        pl.semaphore_signal(barrier, inc=1, device_id={"hist": h, "tsec": tsec}, device_id_type=MESH)
    for h in range(8):
        for odd in range(2):
            source = 2 * hist + odd
            @pl.when(jnp.logical_or(source != tsec, hist != h))
            def _():
                pl.semaphore_signal(barrier, inc=1, device_id={"hist": h, "tsec": source}, device_id_type=MESH)
    pl.semaphore_wait(barrier, jnp.where(target == hist, 18, 19))

    is_last = jnp.where(hist == 7, 1.0, 0.0).astype(f32)

    def remote(src, dst, ss, rs, h):
        return pltpu.make_async_remote_copy(
            src_ref=src, dst_ref=dst, send_sem=ss, recv_sem=rs,
            device_id={"hist": h, "tsec": tsec}, device_id_type=MESH,
        )

    def memory(k, panel):
        top, low = pl.ds(0, HALF), pl.ds(HALF, HALF)

        def chunk(d):
            out = dot(panel[...], green[d])
            re = out[:HALF, :LANES] - out[HALF:, LANES:]
            im = out[HALF:, :LANES] + out[:HALF, LANES:]
            if k == 0:
                tail = green[d, green.shape[1] - HALF :, :].astype(f32) * is_last
                re, im = re + tail[:, :LANES], im + tail[:, LANES:]
            return re, im

        hop_a = remote(sums.at[k, 0, top], hop_recv.at[k, top], hop_ss.at[k, 0], hop_rs.at[k, 0], right)
        hop_b = remote(sums.at[k, 0, low], hop_recv.at[k, low], hop_ss.at[k, 1], hop_rs.at[k, 1], left)
        end_a = remote(sums.at[k, 1], end_recv.at[k, 0], end_ss.at[k, 0], end_rs.at[k, 0], right)
        end_b = remote(sums.at[k, 2], end_recv.at[k, 1], end_ss.at[k, 1], end_rs.at[k, 1], left)

        def step(i, carry):
            o = jnp.where(i == 0, 2, jnp.where(i == 1, 1, jnp.where(i == 2, 3, 0)))
            base = ((chip + o) % 4) * 2
            far, near = base + 1 - core, base + core
            if k == 0:
                for copy in loads(far):
                    copy.wait()
            re, im = chunk(far)
            sib_send[k, i, :HALF] = re
            sib_send[k, i, HALF:] = im
            swap = remote(sib_send.at[k, i], sib_recv.at[k, i], sib_ss.at[k, i], sib_rs.at[k, i], sibling)
            swap.start()
            if k == 0:
                for copy in loads(near):
                    copy.wait()
            re, im = chunk(near)
            swap.wait()
            sums[k, i, :HALF] = re + sib_recv[k, i, :HALF]
            sums[k, i, HALF:] = im + sib_recv[k, i, HALF:]

            @pl.when(i == 0)
            def _():
                hop_a.start()
                hop_b.start()

            @pl.when(i == 1)
            def _():
                hop_a.wait_recv()
                sums[k, 1, :HALF] = sums[k, 1, :HALF] + hop_recv[k, :HALF]
                end_a.start()

            @pl.when(i == 2)
            def _():
                hop_b.wait_recv()
                sums[k, 2, HALF:] = sums[k, 2, HALF:] + hop_recv[k, HALF:]
                end_b.start()

            return carry

        lax.fori_loop(0, 4, step, 0)
        end_a.wait_recv()
        end_b.wait_recv()
        for copy in (hop_a, hop_b, end_a, end_b):
            copy.wait_send()
        return sums[k, 3] + end_recv[k, 0] + end_recv[k, 1]

    lane_group = lax.broadcasted_iota(i32, (LANES, LANES), 1) // N

    def regroup(pick, store):
        for s in range(4):
            value = None
            for a in range(4):
                moved = pick(a)
                if a != s:
                    moved = pltpu.roll(moved, (N * (a - s)) % LANES, 1)
                value = moved if value is None else jnp.where(lane_group == a, moved, value)
            store(s, value)

    def self_energy(k):
        peak = jnp.maximum(jnp.max(jnp.abs(held[...])), 1e-30)
        scale, unit = PEAK / peak, peak / PEAK

        def store_field(s, value):
            whole = jnp.round(value * scale).astype(i32)
            both = lax.shift_left(whole[:64], 16) | (whole[64:] & 0xFFFF)
            field[s] = both
        regroup(lambda a: held[pl.ds(a, LANES, stride=4), :], store_field)
        for j in range(TILES):
            for s in range(4):
                packed[j, s] = field[s, pl.ds(j, 8, stride=TILES), :]

        def tile(j, carry):
            def term(q, acc):
                values = []
                for f in range(3):
                    pair = pair_ref[j, f * Q + q]
                    low, high = pair & (LANES - 1), lax.shift_right_logical(pair, 7)
                    masks = [high == n for n in range(1, TILES)]
                    parts = []
                    for s in range(4):
                        found = jnp.take_along_axis(packed[0, s], low, axis=1)
                        for n in range(1, TILES):
                            found = jnp.where(masks[n - 1], jnp.take_along_axis(packed[n, s], low, axis=1), found)
                        parts.append((
                            lax.shift_right_arithmetic(found, 16).astype(f32),
                            lax.shift_right_arithmetic(lax.shift_left(found, 16), 16).astype(f32),
                        ))
                    values.append(parts)
                weight = weight_ref[j, q]
                result = []
                for s in range(4):
                    (ar, ai), (br, bi), (cr, ci) = values[0][s], values[1][s], values[2][s]
                    pr, pi = ar * br - ai * bi, ar * bi + ai * br
                    result.append(acc[2 * s] + weight * (pr * cr + pi * ci))
                    result.append(acc[2 * s + 1] + weight * (pi * cr - pr * ci))
                return tuple(result)

            acc = lax.fori_loop(0, Q, term, tuple(jnp.zeros((8, LANES), f32) for _ in range(8)), unroll=2)
            for s in range(4):
                for part in range(2):
                    spread[s, j, part * 8 : part * 8 + 8, :] = acc[2 * s + part] * (unit * unit * unit)
            return carry

        lax.fori_loop(0, TILES, tile, 0)

        def store_sigma(a, value):
            sig[pl.ds(a, LANES, stride=4), :] = value
        for s in range(4):
            for j in range(TILES):
                for part in range(2):
                    held_rows = pl.ds(part * 64 + j, 8, stride=TILES)
                    sib_send[k, s, held_rows, :] = spread[s, j, part * 8 : part * 8 + 8, :]
        regroup(lambda s: sib_send[k, s, :LANES, :], store_sigma)

    def gather_copy(o):
        slot = (tsec % 2) * 8 + hist
        there = panel_next.at[:, pl.ds(pl.multiple_of(slot * LANES, LANES), LANES)]
        return pltpu.make_async_remote_copy(
            src_ref=sigma_out, dst_ref=there, send_sem=gat_ss.at[o], recv_sem=gat_rs.at[slot],
            device_id={"hist": target, "tsec": (tsec + o) % 16}, device_id_type=MESH,
        )

    def own_copy():
        slot = (tsec % 2) * 8 + hist
        there = panel_next.at[:, pl.ds(pl.multiple_of(slot * LANES, LANES), LANES)]
        return pltpu.make_async_copy(sigma_out, there, gat_ls)

    for k in range(NBLK):
        total = memory(k, panel_ref if k == 0 else panel_next)
        rhs = total if k == 0 else total + held[...]
        solved = dot(inv_ref[k], rhs, HIGHEST)
        held[...] = solved
        rows_ref[k] = solved.T
        self_energy(k)
        if k + 1 < NBLK:
            sigma_out[...] = sig[...].astype(bf16)
            for o in range(1, 16):
                gather_copy(o).start()

            @pl.when(target != hist)
            def _():
                gather_copy(0).start()

            @pl.when(target == hist)
            def _():
                own_copy().start()
        sigma_ref[k] = sig[...].T.astype(bf16)
        if k + 1 < NBLK:
            own_slot = (tsec % 2) * 8 + hist
            for slot in range(16):
                there = panel_next.at[:, pl.ds(slot * LANES, LANES)]
                arrived = pltpu.make_async_remote_copy(
                    src_ref=sigma_out, dst_ref=there, send_sem=gat_ss.at[0], recv_sem=gat_rs.at[slot],
                    device_id={"hist": sibling, "tsec": tsec}, device_id_type=MESH,
                )

                @pl.when(jnp.logical_or(target != hist, own_slot != slot))
                def _():
                    arrived.wait_recv()

            @pl.when(target == hist)
            def _():
                own_copy().wait()
            for o in range(1, 16):
                gather_copy(o).wait_send()

            @pl.when(target != hist)
            def _():
                gather_copy(0).wait_send()


def per_device(hist_green, sigma_panel, step_operator, coupling, pair_index):
    inverse = invert(step_operator)
    pairs = pair_index.reshape(3 * Q, TILES, LANES).transpose(1, 0, 2)
    pairs = jnp.broadcast_to(pairs[:, :, None], (TILES, 3 * Q, 8, LANES))
    weights = coupling.reshape(Q, TILES, LANES).transpose(1, 0, 2)
    weights = jnp.broadcast_to(weights[:, :, None], (TILES, Q, 8, LANES))
    panel = sigma_panel.T
    depth = panel.shape[1]
    vmem = pl.BlockSpec(memory_space=pltpu.VMEM)
    dma = pltpu.SemaphoreType.DMA
    rows, sigma = pl.pallas_call(
        window_kernel,
        out_shape=(
            jax.ShapeDtypeStruct((NBLK, LANES, WIDE), f32),
            jax.ShapeDtypeStruct((NBLK, LANES, WIDE), bf16),
        ),
        in_specs=[pl.BlockSpec(memory_space=pl.ANY)] + [vmem] * 4,
        out_specs=(vmem, vmem),
        scratch_shapes=[
            pltpu.VMEM((8, depth, 2 * LANES), bf16),
            pltpu.VMEM((WIDE, depth), bf16),
            pltpu.VMEM((WIDE, LANES), f32),
            pltpu.VMEM((4, 64, LANES), i32),
            pltpu.VMEM((TILES, 4, 8, LANES), i32),
            pltpu.VMEM((4, TILES, 16, LANES), f32),
            pltpu.VMEM((WIDE, LANES), f32),
            pltpu.VMEM((WIDE, LANES), bf16),
            pltpu.VMEM((NBLK, 4, WIDE, LANES), f32),
            pltpu.VMEM((NBLK, 4, WIDE, LANES), f32),
            pltpu.VMEM((NBLK, 4, WIDE, LANES), f32),
            pltpu.VMEM((NBLK, WIDE, LANES), f32),
            pltpu.VMEM((NBLK, 2, WIDE, LANES), f32),
            dma((8, 2)),
            dma((NBLK, 4)), dma((NBLK, 4)),
            dma((NBLK, 2)), dma((NBLK, 2)),
            dma((NBLK, 2)), dma((NBLK, 2)),
            dma((16,)), dma((16,)), dma(()),
        ],
        compiler_params=pltpu.CompilerParams(
            collective_id=0, has_side_effects=True, vmem_limit_bytes=56 << 20
        ),
    )(hist_green, panel, inverse, pairs, weights)
    return rows[:, None], sigma[:, None]


def solution(mesh):
    return jax.shard_map(
        per_device,
        mesh=mesh,
        in_specs=(P(None, "hist", "tsec"), P("hist", None), P(), P(), P()),
        out_specs=(P(None, "tsec", "hist", None), P(None, "tsec", "hist", None)),
        check_vma=False,
    )
```

```python
import functools

import jax
import jax.numpy as jnp
from jax import lax
from jax.experimental import pallas as pl
from jax.experimental.pallas import tpu as pltpu
from jax.sharding import PartitionSpec as P

N = 32
B = 8
NBLK = 2
Q = 8
HALF = B * N
WIDE = 2 * HALF
LANES = 128
PAIRS = N * N
TILES = PAIRS // LANES
MESH = pl.DeviceIdType.MESH
f32, bf16, i32 = jnp.float32, jnp.bfloat16, jnp.int32
HIGHEST = lax.Precision.HIGHEST
PEAK = 32000.0


def dot(left, right, precision=None):
    return jnp.dot(left, right, preferred_element_type=f32, precision=precision)


def inverse_kernel(op_ref, out_ref, x_ref, r_ref):
    block = pl.program_id(0)
    rows = lax.broadcasted_iota(i32, (HALF, HALF), 0)
    cols = lax.broadcasted_iota(i32, (HALF, HALF), 1)
    eye = jnp.where(rows == cols, 1.0, 0.0).astype(f32)
    ar, ai = op_ref[block, 0], op_ref[block, 1]
    inv_row = 1.0 / jnp.sum(ar * eye, axis=0, keepdims=True)
    inv_col = 1.0 / jnp.sum(ar * eye, axis=1, keepdims=True)
    x_ref[0] = inv_col * (eye + (eye - ar * inv_row))
    x_ref[1] = inv_col * (-ai * inv_row)

    def residual():
        ar, ai, xr, xi = op_ref[block, 0], op_ref[block, 1], x_ref[0], x_ref[1]
        r_ref[0] = eye - (dot(ar, xr, HIGHEST) - dot(ai, xi, HIGHEST))
        r_ref[1] = -(dot(ar, xi, HIGHEST) + dot(ai, xr, HIGHEST))
        return jnp.max(jnp.sum(jnp.abs(r_ref[0]) + jnp.abs(r_ref[1]), axis=0, keepdims=True))

    def improve(precision):
        xr, xi, rr, ri = x_ref[0], x_ref[1], r_ref[0], r_ref[1]
        x_ref[0] = xr + (dot(xr, rr, precision) - dot(xi, ri, precision))
        x_ref[1] = xi + (dot(xr, ri, precision) + dot(xi, rr, precision))

    def unfinished(carry):
        step, norm = carry
        return jnp.logical_and(step < 40, norm > 3e-3)

    def again(carry):
        improve(HIGHEST)
        return carry[0] + 1, residual()

    lax.while_loop(unfinished, again, (jnp.int32(0), residual()))
    improve(None)
    xr, xi = x_ref[0], x_ref[1]
    out_ref[0, :HALF, :HALF] = xr
    out_ref[0, :HALF, HALF:] = -xi
    out_ref[0, HALF:, :HALF] = xi
    out_ref[0, HALF:, HALF:] = xr


def invert(step_operator):
    return pl.pallas_call(
        inverse_kernel,
        grid=(NBLK,),
        out_shape=jax.ShapeDtypeStruct((NBLK, WIDE, WIDE), f32),
        in_specs=[pl.BlockSpec(memory_space=pltpu.VMEM)],
        out_specs=pl.BlockSpec((1, WIDE, WIDE), lambda k: (k, 0, 0)),
        scratch_shapes=[pltpu.VMEM((2, HALF, HALF), f32)] * 2,
        compiler_params=pltpu.CompilerParams(vmem_limit_bytes=32 << 20),
    )(step_operator)


def window_kernel(
    green_hbm, panel_hbm, inv_hbm, pair_ref, weight_ref,
    rows_ref, sigma_ref,
    pair_wide, weight_wide,
    green, panel_raw, panel_now, panel_next, inv_ref, held, field, packed, spread, sig, sigma_out,
    sib_send, sib_recv, sums, msg_send, msg_recv, unit_send, unit_recv,
    load_sem, in_sem, sib_ss, sib_rs, msg_ss, msg_rs, unit_ss, unit_rs,
    st_ss, st_rs, st_ls, a1_ss, a1_rs, a2_ss, a2_rs, b1_ss, b1_rs, b2_ss, b2_rs,
):
    hist, tsec = lax.axis_index("hist"), lax.axis_index("tsec")
    chip, core = hist // 2, hist % 2
    z, y = tsec // 4, tsec % 4
    sibling = chip * 2 + 1 - core
    holder = core == y // 2
    depth = panel_now.shape[1]

    def at_chip(o, which):
        return ((chip + o) % 4) * 2 + which

    def loads(d):
        lanes = pl.ds(pl.multiple_of(d * LANES, LANES), LANES)
        return [
            pltpu.make_async_copy(
                green_hbm.at[part, :, lanes],
                green.at[d, :, pl.ds(part * LANES, LANES)],
                load_sem.at[d, part],
            )
            for part in range(2)
        ]

    panel_load = pltpu.make_async_copy(panel_hbm, panel_raw, in_sem.at[0])
    inv_load = pltpu.make_async_copy(inv_hbm, inv_ref, in_sem.at[1])
    panel_load.start()
    for o in (2, 1, 3, 0):
        for d in (at_chip(o, 1 - core), at_chip(o, core)):
            for copy in loads(d):
                copy.start()
    inv_load.start()

    barrier = pltpu.get_barrier_semaphore()

    def greet(h, t):
        pl.semaphore_signal(barrier, inc=1, device_id={"hist": h, "tsec": t}, device_id_type=MESH)

    greet(sibling, tsec)
    for o in range(1, 4):
        greet(at_chip(o, core), tsec)
        greet(hist, z * 4 + (y + o) % 4)
        greet(hist, ((z + o) % 4) * 4 + y)
    for h in range(8):
        @pl.when(jnp.logical_and(holder, jnp.logical_or(hist != h, z != chip)))
        def _():
            greet(h, chip * 4 + y)

    for j in range(TILES):
        lanes = slice(j * LANES, (j + 1) * LANES)
        for r in range(3 * Q):
            pair_wide[j, r] = jnp.broadcast_to(pair_ref[r : r + 1, lanes], (8, LANES))
        for r in range(Q):
            weight_wide[j, r] = jnp.broadcast_to(weight_ref[r : r + 1, lanes], (8, LANES))

    panel_load.wait()
    for r in range(depth // HALF):
        panel_now[:, r * HALF : (r + 1) * HALF] = panel_raw[r * HALF : (r + 1) * HALF, :].T
    own_part = hist == 2 * z + y // 2
    pl.semaphore_wait(barrier, jnp.where(own_part, 13, 14))

    is_last = jnp.where(hist == 7, 1.0, 0.0).astype(f32)

    def remote(src, dst, ss, rs, h, t):
        return pltpu.make_async_remote_copy(
            src_ref=src, dst_ref=dst, send_sem=ss, recv_sem=rs,
            device_id={"hist": h, "tsec": t}, device_id_type=MESH,
        )

    def memory(k, panel):
        def chunk(d):
            out = dot(panel[...], green[d])
            re = out[:HALF, :LANES] - out[HALF:, LANES:]
            im = out[HALF:, :LANES] + out[:HALF, LANES:]
            if k == 0:
                tail = green[d, green.shape[1] - HALF :, :].astype(f32) * is_last
                re, im = re + tail[:, :LANES], im + tail[:, LANES:]
            return re, im

        def swap(i):
            return remote(sib_send.at[k, i], sib_recv.at[k, i], sib_ss.at[k, i], sib_rs.at[k, i], sibling, tsec)

        def messages(o):
            there = at_chip(o, core)
            return (
                remote(msg_send.at[k, o - 1], msg_recv.at[k, o - 1], msg_ss.at[k, o - 1], msg_rs.at[k, o - 1], there, tsec),
                remote(unit_send.at[k, o - 1], unit_recv.at[k, o - 1], unit_ss.at[k, o - 1], unit_rs.at[k, o - 1], there, tsec),
            )

        def offset(i):
            return jnp.where(i == 0, 2, jnp.where(i == 1, 1, jnp.where(i == 2, 3, 0)))

        def step(i, carry):
            @pl.when(i < 4)
            def _():
                far = at_chip(offset(i), 1 - core)
                if k == 0:
                    for copy in loads(far):
                        copy.wait()
                re, im = chunk(far)
                sib_send[k, i, :HALF] = re
                sib_send[k, i, HALF:] = im
                swap(i).start()

            @pl.when(i > 0)
            def _():
                last = i - 1
                swap(last).wait()

                @pl.when(last < 3)
                def _():
                    o = offset(last)
                    re = sums[k, last, :HALF] + sib_recv[k, last, :HALF]
                    im = sums[k, last, HALF:] + sib_recv[k, last, HALF:]
                    peak = jnp.maximum(jnp.max(jnp.maximum(jnp.abs(re), jnp.abs(im))), 1e-30)
                    scale = PEAK / peak
                    high = jnp.round(re * scale).astype(i32)
                    low = jnp.round(im * scale).astype(i32)
                    msg_send[k, o - 1] = lax.shift_left(high, 16) | (low & 0xFFFF)
                    unit_send[k, o - 1] = jnp.full((8, LANES), 1.0, f32) * (peak / PEAK)
                    for copy in messages(o):
                        copy.start()

            @pl.when(i < 4)
            def _():
                near = at_chip(offset(i), core)
                if k == 0:
                    for copy in loads(near):
                        copy.wait()
                re, im = chunk(near)
                sums[k, i, :HALF] = re
                sums[k, i, HALF:] = im

            return carry

        lax.fori_loop(0, 5, step, 0)
        re = sums[k, 3, :HALF] + sib_recv[k, 3, :HALF]
        im = sums[k, 3, HALF:] + sib_recv[k, 3, HALF:]
        for o in (1, 3, 2):
            for copy in messages(o):
                copy.wait()
            both = msg_recv[k, o - 1]
            unit = unit_recv[k, o - 1, :1, :1]
            re = re + lax.shift_right_arithmetic(both, 16).astype(f32) * unit
            im = im + lax.shift_right_arithmetic(lax.shift_left(both, 16), 16).astype(f32) * unit
        return jnp.concatenate([re, im], axis=0)

    lane_group = lax.broadcasted_iota(i32, (LANES, LANES), 1) // N

    def regroup(pick, store):
        for s in range(4):
            value = None
            for a in range(4):
                moved = pick(a)
                if a != s:
                    moved = pltpu.roll(moved, (N * (a - s)) % LANES, 1)
                value = moved if value is None else jnp.where(lane_group == a, moved, value)
            store(s, value)

    def self_energy(k):
        peak = jnp.maximum(jnp.max(jnp.abs(held[...])), 1e-30)
        scale, unit = PEAK / peak, peak / PEAK

        def store_field(s, value):
            whole = jnp.round(value * scale).astype(i32)
            both = lax.shift_left(whole[:64], 16) | (whole[64:] & 0xFFFF)
            field[s] = both
        regroup(lambda a: held[pl.ds(a, LANES, stride=4), :], store_field)
        for j in range(TILES):
            for s in range(4):
                packed[j, s] = field[s, pl.ds(j, 8, stride=TILES), :]

        def tile(j, carry):
            def term(q, acc):
                values = []
                for f in range(3):
                    pair = pair_wide[j, f * Q + q]
                    low, high = pair & (LANES - 1), lax.shift_right_logical(pair, 7)
                    masks = [high == n for n in range(1, TILES)]
                    parts = []
                    for s in range(4):
                        found = jnp.take_along_axis(packed[0, s], low, axis=1)
                        for n in range(1, TILES):
                            found = jnp.where(masks[n - 1], jnp.take_along_axis(packed[n, s], low, axis=1), found)
                        parts.append((
                            lax.shift_right_arithmetic(found, 16).astype(f32),
                            lax.shift_right_arithmetic(lax.shift_left(found, 16), 16).astype(f32),
                        ))
                    values.append(parts)
                weight = weight_wide[j, q]
                result = []
                for s in range(4):
                    (ar, ai), (br, bi), (cr, ci) = values[0][s], values[1][s], values[2][s]
                    pr, pi = ar * br - ai * bi, ar * bi + ai * br
                    result.append(acc[2 * s] + weight * (pr * cr + pi * ci))
                    result.append(acc[2 * s + 1] + weight * (pi * cr - pr * ci))
                return tuple(result)

            acc = lax.fori_loop(0, Q, term, tuple(jnp.zeros((8, LANES), f32) for _ in range(8)), unroll=2)
            for s in range(4):
                for part in range(2):
                    spread[s, j, part * 8 : part * 8 + 8, :] = acc[2 * s + part] * (unit * unit * unit)
            return carry

        lax.fori_loop(0, TILES, tile, 0)

        def store_sigma(a, value):
            sig[pl.ds(a, LANES, stride=4), :] = value
        for s in range(4):
            for j in range(TILES):
                for part in range(2):
                    held_rows = pl.ds(part * 64 + j, 8, stride=TILES)
                    sib_send[k, s, held_rows, :] = spread[s, j, part * 8 : part * 8 + 8, :]
        regroup(lambda s: sib_send[k, s, :LANES, :], store_sigma)

    def first(j):
        slot = pl.ds(pl.multiple_of((y % 2) * 1024 + hist * LANES, LANES), LANES)
        rows = pl.ds(j * LANES, LANES)
        return remote(
            sigma_out.at[rows], panel_next.at[rows, slot], st_ss.at[j], st_rs.at[hist], 2 * z + y // 2, 4 * j + y
        )

    def first_here(j):
        slot = pl.ds(pl.multiple_of((y % 2) * 1024 + hist * LANES, LANES), LANES)
        rows = pl.ds(j * LANES, LANES)
        return pltpu.make_async_copy(sigma_out.at[rows], panel_next.at[rows, slot], st_ls)

    def piece(second, j, odd):
        rows = pl.ds(pl.multiple_of(j * LANES + second * 64, 64), 64)
        return panel_next.at[rows, pl.ds(pl.multiple_of(odd * 1024, 1024), 1024)]

    def pass_on(second, j, odd, ss, rs, t):
        return remote(piece(second, j, odd), piece(second, j, odd), ss, rs, hist, t)

    def along_y(n):
        return z * 4 + (y + n) % 4

    def along_z(n):
        return ((z + n) % 4) * 4 + y

    def a1(n):
        return pass_on(0, z, y % 2, a1_ss.at[n - 1], a1_rs.at[y % 2], along_y(n))

    def b1(n):
        return pass_on(1, z, y % 2, b1_ss.at[n - 1], b1_rs.at[z], along_z(n))

    def a2(odd, n):
        return pass_on(0, z, odd, a2_ss.at[odd, n - 1], a2_rs.at[z, odd], along_z(n))

    def b2(m, n):
        j = (z + m) % 4
        return pass_on(1, j, y % 2, b2_ss.at[m, n - 1], b2_rs.at[j, y % 2], along_y(n))

    def exchange():
        for j in range(4):
            here = jnp.logical_and(own_part, z == j)

            @pl.when(jnp.logical_not(here))
            def _():
                first(j).start()

            @pl.when(here)
            def _():
                first_here(j).start()

    def arrived(second, j, odd, rs):
        pass_on(second, j, odd, a1_ss.at[0], rs, along_y(1)).wait_recv()

    def relay():
        @pl.when(holder)
        def _():
            for h in range(8):
                slot = pl.ds(pl.multiple_of((y % 2) * 1024 + h * LANES, LANES), LANES)
                rows = pl.ds(pl.multiple_of(z * LANES, LANES), LANES)

                @pl.when(jnp.logical_or(hist != h, z != chip))
                def _():
                    remote(
                        sigma_out.at[pl.ds(0, LANES)], panel_next.at[rows, slot], st_ss.at[0], st_rs.at[h], sibling, tsec
                    ).wait_recv()

            for j in range(4):
                @pl.when(jnp.logical_and(own_part, z == j))
                def _():
                    first_here(j).wait()

            for n in (2, 1, 3):
                a1(n).start()
                b1(n).start()
            for n in (2, 1, 3):
                a2(y % 2, n).start()
                b2(0, n).start()

        for odd in range(2):
            @pl.when(2 * core + odd != y)
            def _():
                arrived(0, z, odd, a1_rs.at[odd])
                for n in (2, 1, 3):
                    a2(odd, n).start()

        @pl.when(holder)
        def _():
            for m in (1, 3, 2):
                j = (z + m) % 4
                arrived(1, j, y % 2, b1_rs.at[j])
                for n in (2, 1, 3):
                    b2(m, n).start()

    def settle():
        for odd in range(2):
            for m in (1, 3, 2):
                j = (z + m) % 4
                arrived(0, j, odd, a2_rs.at[j, odd])

            @pl.when(2 * core + odd != y)
            def _():
                for j in range(4):
                    arrived(1, j, odd, b2_rs.at[j, odd])

    def drain():
        for j in range(4):
            @pl.when(jnp.logical_not(jnp.logical_and(own_part, z == j)))
            def _():
                first(j).wait_send()
        for n in range(1, 4):
            for odd in range(2):
                a2(odd, n).wait_send()

        @pl.when(holder)
        def _():
            for n in range(1, 4):
                a1(n).wait_send()
                b1(n).wait_send()
                for m in range(4):
                    b2(m, n).wait_send()

    for k in range(NBLK):
        total = memory(k, panel_now if k == 0 else panel_next)
        rhs = total if k == 0 else total + held[...]
        if k == 0:
            inv_load.wait()
        solved = dot(inv_ref[k], rhs, HIGHEST)
        held[...] = solved
        self_energy(k)
        if k + 1 < NBLK:
            sigma_out[...] = sig[...].astype(bf16)
            exchange()
            relay()
        rows_ref[k] = held[...].T
        sigma_ref[k] = sig[...].T.astype(bf16)
        if k + 1 < NBLK:
            settle()
    drain()


def per_device(hist_green, sigma_panel, step_operator, coupling, pair_index):
    inverse = invert(step_operator)
    pairs = pair_index.reshape(3 * Q, PAIRS)
    depth = sigma_panel.shape[0]
    anywhere = pl.BlockSpec(memory_space=pl.ANY)
    vmem = pl.BlockSpec(memory_space=pltpu.VMEM)
    dma = pltpu.SemaphoreType.DMA
    rows, sigma = pl.pallas_call(
        window_kernel,
        out_shape=(
            jax.ShapeDtypeStruct((NBLK, LANES, WIDE), f32),
            jax.ShapeDtypeStruct((NBLK, LANES, WIDE), bf16),
        ),
        in_specs=[anywhere, anywhere, anywhere, vmem, vmem],
        out_specs=(vmem, vmem),
        scratch_shapes=[
            pltpu.VMEM((TILES, 3 * Q, 8, LANES), i32),
            pltpu.VMEM((TILES, Q, 8, LANES), f32),
            pltpu.VMEM((8, depth, 2 * LANES), bf16),
            pltpu.VMEM((depth, WIDE), bf16),
            pltpu.VMEM((WIDE, depth), bf16),
            pltpu.VMEM((WIDE, depth), bf16),
            pltpu.VMEM((NBLK, WIDE, WIDE), f32),
            pltpu.VMEM((WIDE, LANES), f32),
            pltpu.VMEM((4, 64, LANES), i32),
            pltpu.VMEM((TILES, 4, 8, LANES), i32),
            pltpu.VMEM((4, TILES, 16, LANES), f32),
            pltpu.VMEM((WIDE, LANES), f32),
            pltpu.VMEM((WIDE, LANES), bf16),
            pltpu.VMEM((NBLK, 4, WIDE, LANES), f32),
            pltpu.VMEM((NBLK, 4, WIDE, LANES), f32),
            pltpu.VMEM((NBLK, 4, WIDE, LANES), f32),
            pltpu.VMEM((NBLK, 3, HALF, LANES), i32),
            pltpu.VMEM((NBLK, 3, HALF, LANES), i32),
            pltpu.VMEM((NBLK, 3, 8, LANES), f32),
            pltpu.VMEM((NBLK, 3, 8, LANES), f32),
            dma((8, 2)), dma((2,)),
            dma((NBLK, 4)), dma((NBLK, 4)),
            dma((NBLK, 3)), dma((NBLK, 3)),
            dma((NBLK, 3)), dma((NBLK, 3)),
            dma((4,)), dma((8,)), dma(()),
            dma((3,)), dma((2,)), dma((2, 3)), dma((4, 2)),
            dma((3,)), dma((4,)), dma((4, 3)), dma((4, 2)),
        ],
        compiler_params=pltpu.CompilerParams(
            collective_id=0, has_side_effects=True, vmem_limit_bytes=56 << 20
        ),
    )(hist_green, sigma_panel, inverse, pairs, coupling)
    return rows[:, None], sigma[:, None]


def solution(mesh):
    return jax.shard_map(
        per_device,
        mesh=mesh,
        in_specs=(P(None, "hist", "tsec"), P("hist", None), P(), P(), P()),
        out_specs=(P(None, "tsec", "hist", None), P(None, "tsec", "hist", None)),
        check_vma=False,
    )
```

```python
import functools

import jax
import jax.numpy as jnp
from jax import lax
from jax.experimental import pallas as pl
from jax.experimental.pallas import tpu as pltpu
from jax.sharding import PartitionSpec as P

N = 32
B = 8
NBLK = 2
Q = 8
HALF = B * N
WIDE = 2 * HALF
LANES = 128
PAIRS = N * N
TILES = PAIRS // LANES
MESH = pl.DeviceIdType.MESH
f32, bf16, i32 = jnp.float32, jnp.bfloat16, jnp.int32
HIGHEST = lax.Precision.HIGHEST
PEAK = 32000.0


def dot(left, right, precision=None):
    return jnp.dot(left, right, preferred_element_type=f32, precision=precision)


def inverse_kernel(op_hbm, out_ref, a_ref, x_ref, r_ref, sem):
    load = pltpu.make_async_copy(op_hbm.at[lax.axis_index("hist") % 2], a_ref, sem)
    load.start()
    rows = lax.broadcasted_iota(i32, (HALF, HALF), 0)
    cols = lax.broadcasted_iota(i32, (HALF, HALF), 1)
    eye = jnp.where(rows == cols, 1.0, 0.0).astype(f32)
    load.wait()
    ar, ai = a_ref[0], a_ref[1]
    inv_row = 1.0 / jnp.sum(ar * eye, axis=0, keepdims=True)
    inv_col = 1.0 / jnp.sum(ar * eye, axis=1, keepdims=True)
    x_ref[:, :HALF] = inv_col * (eye + (eye - ar * inv_row))
    x_ref[:, HALF:] = inv_col * (-ai * inv_row)

    def product(left, right, precision):
        out = dot(left, right, precision)
        return out[:HALF, :HALF] - out[HALF:, HALF:], out[:HALF, HALF:] + out[HALF:, :HALF]

    def residual():
        re, im = product(a_ref[...].reshape(WIDE, HALF), x_ref[...], HIGHEST)
        re, im = eye - re, -im
        r_ref[:, :HALF] = re
        r_ref[:, HALF:] = im
        return jnp.max(jnp.sum(jnp.abs(re) + jnp.abs(im), axis=0, keepdims=True))

    def improve(precision):
        left = jnp.concatenate([x_ref[:, :HALF], x_ref[:, HALF:]], axis=0)
        re, im = product(left, r_ref[...], precision)
        x_ref[:, :HALF] = x_ref[:, :HALF] + re
        x_ref[:, HALF:] = x_ref[:, HALF:] + im

    def unfinished(carry):
        step, norm = carry
        return jnp.logical_and(step < 40, norm > 3e-3)

    def again(carry):
        improve(HIGHEST)
        return carry[0] + 1, residual()

    lax.while_loop(unfinished, again, (jnp.int32(0), residual()))
    improve(None)
    for part in range(2):
        value = x_ref[:, part * HALF : (part + 1) * HALF]
        high = value.astype(bf16)
        out_ref[part * HALF : (part + 1) * HALF] = high
        out_ref[WIDE + part * HALF : WIDE + (part + 1) * HALF] = (value - high.astype(f32)).astype(bf16)


def invert(step_operator):
    return pl.pallas_call(
        inverse_kernel,
        out_shape=jax.ShapeDtypeStruct((2 * WIDE, HALF), bf16),
        in_specs=[pl.BlockSpec(memory_space=pl.ANY)],
        out_specs=pl.BlockSpec(memory_space=pltpu.VMEM),
        scratch_shapes=[
            pltpu.VMEM((2, HALF, HALF), f32),
            pltpu.VMEM((HALF, WIDE), f32),
            pltpu.VMEM((HALF, WIDE), f32),
            pltpu.SemaphoreType.DMA(()),
        ],
        compiler_params=pltpu.CompilerParams(vmem_limit_bytes=32 << 20),
    )(step_operator)


def window_kernel(
    green_hbm, panel_hbm, inv_in, pair_ref, weight_ref,
    rows_ref, sigma_ref,
    pair_wide, weight_wide,
    green, panel_raw, panel_now, panel_next, inv_ref, held, field, packed, spread, wide, half_sig, sig, sigma_out,
    sib_send, sib_recv, sums, msg_send, msg_recv, unit_send, unit_recv,
    load_sem, in_sem, inv_ss, inv_rs, sib_ss, sib_rs, msg_ss, msg_rs, unit_ss, unit_rs,
    st_ss, st_rs, st_ls, a1_ss, a1_rs, a2_ss, a2_rs, b1_ss, b1_rs, b2_ss, b2_rs,
):
    hist, tsec = lax.axis_index("hist"), lax.axis_index("tsec")
    chip, core = hist // 2, hist % 2
    z, y = tsec // 4, tsec % 4
    sibling = chip * 2 + 1 - core
    holder = core == y // 2
    depth = panel_now.shape[1]

    def at_chip(o, which):
        return ((chip + o) % 4) * 2 + which

    def loads(d):
        lanes = pl.ds(pl.multiple_of(d * LANES, LANES), LANES)
        return [
            pltpu.make_async_copy(
                green_hbm.at[part, :, lanes],
                green.at[d, :, pl.ds(part * LANES, LANES)],
                load_sem.at[d, part],
            )
            for part in range(2)
        ]

    panel_load = pltpu.make_async_copy(panel_hbm, panel_raw, in_sem.at[0])
    inv_keep = pltpu.make_async_copy(inv_in, inv_ref.at[core], in_sem.at[1])
    panel_load.start()
    for o in (2, 1, 3, 0):
        for d in (at_chip(o, 1 - core), at_chip(o, core)):
            for copy in loads(d):
                copy.start()
    inv_keep.start()

    barrier = pltpu.get_barrier_semaphore()

    def greet(h, t):
        pl.semaphore_signal(barrier, inc=1, device_id={"hist": h, "tsec": t}, device_id_type=MESH)

    greet(sibling, tsec)
    for o in range(1, 4):
        greet(at_chip(o, core), tsec)
        greet(hist, z * 4 + (y + o) % 4)
        greet(hist, ((z + o) % 4) * 4 + y)
    for h in range(8):
        @pl.when(jnp.logical_and(holder, jnp.logical_or(hist != h, z != chip)))
        def _():
            greet(h, chip * 4 + y)

    for j in range(TILES):
        lanes = slice(j * LANES, (j + 1) * LANES)
        for r in range(3 * Q):
            pair_wide[j, r] = jnp.broadcast_to(pair_ref[r : r + 1, lanes], (8, LANES))
        for r in range(Q):
            weight_wide[j, r] = jnp.broadcast_to(weight_ref[r : r + 1, lanes], (8, LANES))

    panel_load.wait()
    for r in range(depth // HALF):
        panel_now[:, r * HALF : (r + 1) * HALF] = panel_raw[r * HALF : (r + 1) * HALF, :].T
    own_part = hist == 2 * z + y // 2
    is_last = jnp.where(hist == 7, 1.0, 0.0).astype(f32)

    def remote(src, dst, ss, rs, h, t):
        return pltpu.make_async_remote_copy(
            src_ref=src, dst_ref=dst, send_sem=ss, recv_sem=rs,
            device_id={"hist": h, "tsec": t}, device_id_type=MESH,
        )

    inv_give = remote(inv_in, inv_ref.at[core], inv_ss, inv_rs, sibling, tsec)
    inv_take = remote(inv_in, inv_ref.at[1 - core], inv_ss, inv_rs, sibling, tsec)

    def memory(run):
        k = min(run, 1)
        count = WIDE if run == 0 else HALF
        half = count // 2
        base = HALF if run == 2 else 0
        upper, lower = pl.ds(base, half), pl.ds(base + half, half)
        whole, msg_rows = pl.ds(base, count), pl.ds(base // 2, half)

        def chunk(d):
            left = panel_now[...] if run == 0 else panel_next[base : base + count, :]
            out = dot(left, green[d])
            re = out[:half, :LANES] - out[half:, LANES:]
            im = out[half:, :LANES] + out[:half, LANES:]
            if k == 0:
                tail = green[d, green.shape[1] - HALF :, :].astype(f32) * is_last
                re, im = re + tail[:, :LANES], im + tail[:, LANES:]
            return re, im

        def swap(i):
            return remote(
                sib_send.at[k, i, whole], sib_recv.at[k, i, whole], sib_ss.at[run, i], sib_rs.at[run, i], sibling, tsec
            )

        def messages(o):
            there, n = at_chip(o, core), o - 1
            return (
                remote(msg_send.at[k, n, msg_rows], msg_recv.at[k, n, msg_rows], msg_ss.at[run, n], msg_rs.at[run, n], there, tsec),
                remote(unit_send.at[run, n], unit_recv.at[run, n], unit_ss.at[run, n], unit_rs.at[run, n], there, tsec),
            )

        def offset(i):
            return jnp.where(i == 0, 2, jnp.where(i == 1, 1, jnp.where(i == 2, 3, 0)))

        def finish(last):
            swap(last).wait()
            o = offset(last)
            re = sums[k, last, upper] + sib_recv[k, last, upper]
            im = sums[k, last, lower] + sib_recv[k, last, lower]
            peak = jnp.maximum(jnp.max(jnp.maximum(jnp.abs(re), jnp.abs(im))), 1e-30)
            scale = PEAK / peak
            high = jnp.round(re * scale).astype(i32)
            low = jnp.round(im * scale).astype(i32)
            msg_send[k, o - 1, msg_rows] = lax.shift_left(high, 16) | (low & 0xFFFF)
            unit_send[run, o - 1] = jnp.full((8, LANES), 1.0, f32) * (peak / PEAK)
            for copy in messages(o):
                copy.start()

        late = 1 if k == 0 else 0

        def step(i, carry):
            far = at_chip(offset(i), 1 - core)
            if k == 0:
                for copy in loads(far):
                    copy.wait()
            re, im = chunk(far)
            sib_send[k, i, upper] = re
            sib_send[k, i, lower] = im
            if k == 0:
                @pl.when(i == 1)
                def _():
                    pl.semaphore_wait(barrier, jnp.where(own_part, 13, 14))
                    swap(0).start()

                @pl.when(i >= 1)
                def _():
                    swap(i).start()

                @pl.when(i == 3)
                def _():
                    inv_give.start()
            else:
                swap(i).start()

            @pl.when(i > late)
            def _():
                finish(i - 1 - late)

            near = at_chip(offset(i), core)
            if k == 0:
                for copy in loads(near):
                    copy.wait()
            re, im = chunk(near)
            sums[k, i, upper] = re
            sums[k, i, lower] = im
            return carry

        lax.fori_loop(0, 4, step, 0)
        for last in range(3 - late, 3):
            finish(last)
        swap(3).wait()

        def collect():
            re = sums[k, 3, upper] + sib_recv[k, 3, upper]
            im = sums[k, 3, lower] + sib_recv[k, 3, lower]
            for o in (1, 3, 2):
                for copy in messages(o):
                    copy.wait()
                both = msg_recv[k, o - 1, msg_rows]
                unit = unit_recv[run, o - 1, :1, :1]
                re = re + lax.shift_right_arithmetic(both, 16).astype(f32) * unit
                im = im + lax.shift_right_arithmetic(lax.shift_left(both, 16), 16).astype(f32) * unit
            return re, im

        return collect

    def regroup(count, pick, store):
        lane_group = lax.broadcasted_iota(i32, (count, LANES), 1) // N
        for s in range(4):
            value = None
            for a in range(4):
                moved = pick(a)
                if a != s:
                    moved = pltpu.roll(moved, (N * (a - s)) % LANES, 1)
                value = moved if value is None else jnp.where(lane_group == a, moved, value)
            store(s, value)

    def self_energy():
        peak = jnp.maximum(jnp.max(jnp.abs(held[...])), 1e-30)
        scale, unit = PEAK / peak, peak / PEAK

        def store_field(s, value):
            whole = jnp.round(value * scale).astype(i32)
            both = lax.shift_left(whole[:64], 16) | (whole[64:] & 0xFFFF)
            field[s] = both
        regroup(LANES, lambda a: held[pl.ds(a, LANES, stride=4), :], store_field)
        for j in range(TILES):
            for s in range(4):
                packed[j, s] = field[s, pl.ds(j, 8, stride=TILES), :]

        def tile(j, carry):
            def term(q, acc):
                values = []
                for f in range(3):
                    pair = pair_wide[j, f * Q + q]
                    low, high = pair & (LANES - 1), lax.shift_right_logical(pair, 7)
                    masks = [high == n for n in range(1, TILES)]
                    parts = []
                    for s in range(4):
                        found = jnp.take_along_axis(packed[0, s], low, axis=1)
                        for n in range(1, TILES):
                            found = jnp.where(masks[n - 1], jnp.take_along_axis(packed[n, s], low, axis=1), found)
                        parts.append((
                            lax.shift_right_arithmetic(found, 16).astype(f32),
                            lax.shift_right_arithmetic(lax.shift_left(found, 16), 16).astype(f32),
                        ))
                    values.append(parts)
                weight = weight_wide[j, q]
                result = []
                for s in range(4):
                    (ar, ai), (br, bi), (cr, ci) = values[0][s], values[1][s], values[2][s]
                    pr, pi = ar * br - ai * bi, ar * bi + ai * br
                    result.append(acc[2 * s] + weight * (pr * cr + pi * ci))
                    result.append(acc[2 * s + 1] + weight * (pi * cr - pr * ci))
                return tuple(result)

            acc = lax.fori_loop(0, Q, term, tuple(jnp.zeros((8, LANES), f32) for _ in range(8)), unroll=4)
            for s in range(4):
                for part in range(2):
                    spread[s, j, part * 8 : part * 8 + 8, :] = acc[2 * s + part] * (unit * unit * unit)
            return carry

        def tiles(start, stop):
            lax.fori_loop(start, stop, tile, 0)

        def store_piece(a, value):
            half_sig[pl.ds(a, 64, stride=4), :] = value

        def collect(p, share):
            for s in range(4):
                for jj in range(4):
                    for part in range(2):
                        wide[s, pl.ds(part * 32 + jj, 8, stride=4), :] = spread[s, p * 4 + jj, part * 8 : part * 8 + 8, :]
            regroup(64, lambda s: wide[s], store_piece)
            if share:
                sigma_out[p * HALF : (p + 1) * HALF] = half_sig[...].astype(bf16)
            for n in range(16):
                sig[n * N + p * 16 : n * N + p * 16 + 16] = half_sig[n * 16 : n * 16 + 16]

        return tiles, collect

    def first(p, j):
        slot = pl.ds(pl.multiple_of((y % 2) * 1024 + hist * LANES, LANES), LANES)
        rows = pl.ds(p * HALF + j * 64, 64)
        return remote(
            sigma_out.at[rows], panel_next.at[rows, slot], st_ss.at[p, j], st_rs.at[p, hist], 2 * z + y // 2, 4 * j + y
        )

    def first_here(p, j):
        slot = pl.ds(pl.multiple_of((y % 2) * 1024 + hist * LANES, LANES), LANES)
        rows = pl.ds(p * HALF + j * 64, 64)
        return pltpu.make_async_copy(sigma_out.at[rows], panel_next.at[rows, slot], st_ls.at[p])

    def piece(p, second, j, odd):
        rows = pl.ds(pl.multiple_of(p * HALF + j * 64 + second * 32, 32), 32)
        return panel_next.at[rows, pl.ds(pl.multiple_of(odd * 1024, 1024), 1024)]

    def pass_on(p, second, j, odd, ss, rs, t):
        return remote(piece(p, second, j, odd), piece(p, second, j, odd), ss, rs, hist, t)

    def along_y(n):
        return z * 4 + (y + n) % 4

    def along_z(n):
        return ((z + n) % 4) * 4 + y

    def a1(p, n):
        return pass_on(p, 0, z, y % 2, a1_ss.at[p, n - 1], a1_rs.at[p, y % 2], along_y(n))

    def b1(p, n):
        return pass_on(p, 1, z, y % 2, b1_ss.at[p, n - 1], b1_rs.at[p, z], along_z(n))

    def a2(p, odd, n):
        return pass_on(p, 0, z, odd, a2_ss.at[p, odd, n - 1], a2_rs.at[p, z, odd], along_z(n))

    def b2(p, m, n):
        j = (z + m) % 4
        return pass_on(p, 1, j, y % 2, b2_ss.at[p, m, n - 1], b2_rs.at[p, j, y % 2], along_y(n))

    def exchange(p):
        for j in range(4):
            here = jnp.logical_and(own_part, z == j)

            @pl.when(jnp.logical_not(here))
            def _():
                first(p, j).start()

            @pl.when(here)
            def _():
                first_here(p, j).start()

    def arrived(p, second, j, odd, rs):
        pass_on(p, second, j, odd, a1_ss.at[p, 0], rs, along_y(1)).wait_recv()

    def relay_first(p):
        @pl.when(holder)
        def _():
            for h in range(8):
                slot = pl.ds(pl.multiple_of((y % 2) * 1024 + h * LANES, LANES), LANES)
                rows = pl.ds(pl.multiple_of(p * HALF + z * 64, 64), 64)

                @pl.when(jnp.logical_or(hist != h, z != chip))
                def _():
                    remote(
                        sigma_out.at[pl.ds(0, 64)], panel_next.at[rows, slot], st_ss.at[p, 0], st_rs.at[p, h], sibling, tsec
                    ).wait_recv()

            for j in range(4):
                @pl.when(jnp.logical_and(own_part, z == j))
                def _():
                    first_here(p, j).wait()

            for n in (2, 1, 3):
                a1(p, n).start()
                b1(p, n).start()
            for n in (2, 1, 3):
                a2(p, y % 2, n).start()
                b2(p, 0, n).start()

    def relay_second(p):
        for odd in range(2):
            @pl.when(2 * core + odd != y)
            def _():
                arrived(p, 0, z, odd, a1_rs.at[p, odd])
                for n in (2, 1, 3):
                    a2(p, odd, n).start()

        @pl.when(holder)
        def _():
            for m in (1, 3, 2):
                j = (z + m) % 4
                arrived(p, 1, j, y % 2, b1_rs.at[p, j])
                for n in (2, 1, 3):
                    b2(p, m, n).start()

    def settle(p):
        for odd in range(2):
            for m in (1, 3, 2):
                j = (z + m) % 4
                arrived(p, 0, j, odd, a2_rs.at[p, j, odd])

            @pl.when(2 * core + odd != y)
            def _():
                for j in range(4):
                    arrived(p, 1, j, odd, b2_rs.at[p, j, odd])

    def drain(p):
        for j in range(4):
            @pl.when(jnp.logical_not(jnp.logical_and(own_part, z == j)))
            def _():
                first(p, j).wait_send()
        for n in range(1, 4):
            for odd in range(2):
                a2(p, odd, n).wait_send()

        @pl.when(holder)
        def _():
            for n in range(1, 4):
                a1(p, n).wait_send()
                b1(p, n).wait_send()
                for m in range(4):
                    b2(p, m, n).wait_send()

    def solve(k, rhs):
        both = jnp.concatenate([rhs[:HALF], rhs[HALF:]], axis=1)
        high = both.astype(bf16)
        low = (both - high.astype(f32)).astype(bf16)
        out = dot(inv_ref[k], high)
        out = out[:WIDE] + out[WIDE:] + dot(inv_ref[k, :WIDE], low)
        held[:HALF] = out[:HALF, :LANES] - out[HALF:, LANES:]
        held[HALF:] = out[HALF:, :LANES] + out[:HALF, LANES:]

    re, im = memory(0)()
    inv_keep.wait()
    inv_take.wait_recv()
    solve(0, jnp.concatenate([re, im], axis=0))
    tiles, collect = self_energy()
    tiles(0, 4)
    collect(0, True)
    exchange(0)
    tiles(4, 6)
    relay_first(0)
    tiles(6, 8)
    collect(1, True)
    exchange(1)
    relay_second(0)
    rows_ref[0] = held[...].T
    sigma_ref[0] = sig[...].T.astype(bf16)
    relay_first(1)
    relay_second(1)
    settle(0)
    results = [memory(1)]
    settle(1)
    results.append(memory(2))
    for p in range(2):
        re, im = results[p]()
        for n in range(8):
            for part, value in enumerate((re, im)):
                at = part * HALF + n * N + p * 16
                held[at : at + 16] = held[at : at + 16] + value[n * 16 : n * 16 + 16]
    solve(1, held[...])
    tiles, collect = self_energy()
    rows_ref[1] = held[...].T
    tiles(0, 8)
    collect(0, False)
    collect(1, False)
    sigma_ref[1] = sig[...].T.astype(bf16)
    inv_give.wait_send()
    for p in range(2):
        drain(p)


def per_device(hist_green, sigma_panel, step_operator, coupling, pair_index):
    inverse = invert(step_operator)
    pairs = pair_index.reshape(3 * Q, PAIRS)
    depth = sigma_panel.shape[0]
    anywhere = pl.BlockSpec(memory_space=pl.ANY)
    vmem = pl.BlockSpec(memory_space=pltpu.VMEM)
    dma = pltpu.SemaphoreType.DMA
    rows, sigma = pl.pallas_call(
        window_kernel,
        out_shape=(
            jax.ShapeDtypeStruct((NBLK, LANES, WIDE), f32),
            jax.ShapeDtypeStruct((NBLK, LANES, WIDE), bf16),
        ),
        in_specs=[anywhere, anywhere, vmem, vmem, vmem],
        out_specs=(vmem, vmem),
        scratch_shapes=[
            pltpu.VMEM((TILES, 3 * Q, 8, LANES), i32),
            pltpu.VMEM((TILES, Q, 8, LANES), f32),
            pltpu.VMEM((8, depth, 2 * LANES), bf16),
            pltpu.VMEM((depth, WIDE), bf16),
            pltpu.VMEM((WIDE, depth), bf16),
            pltpu.VMEM((WIDE, depth), bf16),
            pltpu.VMEM((NBLK, 2 * WIDE, HALF), bf16),
            pltpu.VMEM((WIDE, LANES), f32),
            pltpu.VMEM((4, 64, LANES), i32),
            pltpu.VMEM((TILES, 4, 8, LANES), i32),
            pltpu.VMEM((4, TILES, 16, LANES), f32),
            pltpu.VMEM((4, 64, LANES), f32),
            pltpu.VMEM((HALF, LANES), f32),
            pltpu.VMEM((WIDE, LANES), f32),
            pltpu.VMEM((WIDE, LANES), bf16),
            pltpu.VMEM((NBLK, 4, WIDE, LANES), f32),
            pltpu.VMEM((NBLK, 4, WIDE, LANES), f32),
            pltpu.VMEM((NBLK, 4, WIDE, LANES), f32),
            pltpu.VMEM((NBLK, 3, HALF, LANES), i32),
            pltpu.VMEM((NBLK, 3, HALF, LANES), i32),
            pltpu.VMEM((3, 3, 8, LANES), f32),
            pltpu.VMEM((3, 3, 8, LANES), f32),
            dma((8, 2)), dma((2,)), dma(()), dma(()),
            dma((3, 4)), dma((3, 4)),
            dma((3, 3)), dma((3, 3)),
            dma((3, 3)), dma((3, 3)),
            dma((2, 4)), dma((2, 8)), dma((2,)),
            dma((2, 3)), dma((2, 2)), dma((2, 2, 3)), dma((2, 4, 2)),
            dma((2, 3)), dma((2, 4)), dma((2, 4, 3)), dma((2, 4, 2)),
        ],
        compiler_params=pltpu.CompilerParams(
            collective_id=0, has_side_effects=True, vmem_limit_bytes=56 << 20
        ),
    )(hist_green, sigma_panel, inverse, pairs, coupling)
    return rows[:, None], sigma[:, None]


def solution(mesh):
    return jax.shard_map(
        per_device,
        mesh=mesh,
        in_specs=(P(None, "hist", "tsec"), P("hist", None), P(), P(), P()),
        out_specs=(P(None, "tsec", "hist", None), P(None, "tsec", "hist", None)),
        check_vma=False,
    )
```

```python
import functools

import jax
import jax.numpy as jnp
from jax import lax
from jax.experimental import pallas as pl
from jax.experimental.pallas import tpu as pltpu
from jax.sharding import PartitionSpec as P

N = 32
B = 8
NBLK = 2
Q = 8
HALF = B * N
WIDE = 2 * HALF
LANES = 128
PAIRS = N * N
TILES = PAIRS // LANES
MESH = pl.DeviceIdType.MESH
f32, bf16, i32 = jnp.float32, jnp.bfloat16, jnp.int32
HIGHEST = lax.Precision.HIGHEST
PEAK = 32000.0


def dot(left, right, precision=None):
    return jnp.dot(left, right, preferred_element_type=f32, precision=precision)


def prepare_kernel(op_ref, pair_ref, weight_ref, out_ref, pair_wide, weight_wide, x_ref, r_ref):
    a_ref = op_ref.at[lax.axis_index("hist") % 2]
    rows = lax.broadcasted_iota(i32, (HALF, HALF), 0)
    cols = lax.broadcasted_iota(i32, (HALF, HALF), 1)
    eye = jnp.where(rows == cols, 1.0, 0.0).astype(f32)
    ar, ai = a_ref[0], a_ref[1]
    inv_row = 1.0 / jnp.sum(ar * eye, axis=0, keepdims=True)
    inv_col = 1.0 / jnp.sum(ar * eye, axis=1, keepdims=True)
    x_ref[:, :HALF] = inv_col * (eye + (eye - ar * inv_row))
    x_ref[:, HALF:] = inv_col * (-ai * inv_row)

    def product(left, right, precision):
        out = dot(left, right, precision)
        return out[:HALF, :HALF] - out[HALF:, HALF:], out[:HALF, HALF:] + out[HALF:, :HALF]

    def residual():
        re, im = product(a_ref[...].reshape(WIDE, HALF), x_ref[...], HIGHEST)
        re, im = eye - re, -im
        r_ref[:, :HALF] = re
        r_ref[:, HALF:] = im
        return jnp.max(jnp.sum(jnp.abs(re) + jnp.abs(im), axis=0, keepdims=True))

    def improve(precision):
        left = jnp.concatenate([x_ref[:, :HALF], x_ref[:, HALF:]], axis=0)
        re, im = product(left, r_ref[...], precision)
        x_ref[:, :HALF] = x_ref[:, :HALF] + re
        x_ref[:, HALF:] = x_ref[:, HALF:] + im

    def unfinished(carry):
        step, norm = carry
        return jnp.logical_and(step < 40, norm > 3e-3)

    def again(carry):
        improve(HIGHEST)
        return carry[0] + 1, residual()

    lax.while_loop(unfinished, again, (jnp.int32(0), residual()))
    improve(None)
    for part in range(2):
        value = x_ref[:, part * HALF : (part + 1) * HALF]
        high = value.astype(bf16)
        out_ref[part * HALF : (part + 1) * HALF] = high
        out_ref[WIDE + part * HALF : WIDE + (part + 1) * HALF] = (value - high.astype(f32)).astype(bf16)
    for j in range(TILES):
        lanes = slice(j * LANES, (j + 1) * LANES)
        for r in range(3 * Q):
            pair_wide[j, r] = jnp.broadcast_to(pair_ref[r : r + 1, lanes], (8, LANES))
        for r in range(Q):
            weight_wide[j, r] = jnp.broadcast_to(weight_ref[r : r + 1, lanes], (8, LANES))


def prepare(step_operator, pairs, coupling):
    vmem = pl.BlockSpec(memory_space=pltpu.VMEM)
    return pl.pallas_call(
        prepare_kernel,
        out_shape=(
            jax.ShapeDtypeStruct((2 * WIDE, HALF), bf16),
            jax.ShapeDtypeStruct((TILES, 3 * Q, 8, LANES), i32),
            jax.ShapeDtypeStruct((TILES, Q, 8, LANES), f32),
        ),
        in_specs=[vmem] * 3,
        out_specs=(vmem,) * 3,
        scratch_shapes=[pltpu.VMEM((HALF, WIDE), f32), pltpu.VMEM((HALF, WIDE), f32)],
        compiler_params=pltpu.CompilerParams(vmem_limit_bytes=32 << 20),
    )(step_operator, pairs, coupling)


def regroup(count, pick, store):
    lane_group = lax.broadcasted_iota(i32, (count, LANES), 1) // N
    for s in range(4):
        value = None
        for a in range(4):
            moved = pick(a)
            if a != s:
                moved = pltpu.roll(moved, (N * (a - s)) % LANES, 1)
            value = moved if value is None else jnp.where(lane_group == a, moved, value)
        store(s, value)


def self_energy(held, sigma_out, pair_wide, weight_wide, field, packed, spread, wide, half_sig, sig):
    peak = jnp.maximum(jnp.max(jnp.abs(held[...])), 1e-30)
    scale, unit = PEAK / peak, peak / PEAK

    def store_field(s, value):
        whole = jnp.round(value * scale).astype(i32)
        both = lax.shift_left(whole[:64], 16) | (whole[64:] & 0xFFFF)
        field[s] = both
    regroup(LANES, lambda a: held[pl.ds(a, LANES, stride=4), :], store_field)
    for j in range(TILES):
        for s in range(4):
            packed[j, s] = field[s, pl.ds(j, 8, stride=TILES), :]

    def tile(j, carry):
        def term(q, acc):
            values = []
            for f in range(3):
                pair = pair_wide[j, f * Q + q]
                low, high = pair & (LANES - 1), lax.shift_right_logical(pair, 7)
                masks = [high == n for n in range(1, TILES)]
                parts = []
                for s in range(4):
                    found = jnp.take_along_axis(packed[0, s], low, axis=1)
                    for n in range(1, TILES):
                        found = jnp.where(masks[n - 1], jnp.take_along_axis(packed[n, s], low, axis=1), found)
                    parts.append((
                        lax.shift_right_arithmetic(found, 16).astype(f32),
                        lax.shift_right_arithmetic(lax.shift_left(found, 16), 16).astype(f32),
                    ))
                values.append(parts)
            weight = weight_wide[j, q]
            result = []
            for s in range(4):
                (ar, ai), (br, bi), (cr, ci) = values[0][s], values[1][s], values[2][s]
                pr, pi = ar * br - ai * bi, ar * bi + ai * br
                result.append(acc[2 * s] + weight * (pr * cr + pi * ci))
                result.append(acc[2 * s + 1] + weight * (pi * cr - pr * ci))
            return tuple(result)

        acc = lax.fori_loop(0, Q, term, tuple(jnp.zeros((8, LANES), f32) for _ in range(8)), unroll=8)
        for s in range(4):
            for part in range(2):
                spread[s, j, part * 8 : part * 8 + 8, :] = acc[2 * s + part] * (unit * unit * unit)
        return carry

    def tiles(start, stop):
        lax.fori_loop(start, stop, tile, 0)

    def store_piece(a, value):
        half_sig[pl.ds(a, 64, stride=4), :] = value

    def collect(p, share):
        for s in range(4):
            for jj in range(4):
                for part in range(2):
                    wide[s, pl.ds(part * 32 + jj, 8, stride=4), :] = spread[s, p * 4 + jj, part * 8 : part * 8 + 8, :]
        regroup(64, lambda s: wide[s], store_piece)
        if share:
            sigma_out[p * HALF : (p + 1) * HALF] = half_sig[...].astype(bf16)
        for n in range(16):
            sig[n * N + p * 16 : n * N + p * 16 + 16] = half_sig[n * 16 : n * 16 + 16]

    return tiles, collect


ENERGY_SCRATCH = [
    pltpu.VMEM((4, 64, LANES), i32),
    pltpu.VMEM((TILES, 4, 8, LANES), i32),
    pltpu.VMEM((4, TILES, 16, LANES), f32),
    pltpu.VMEM((4, 64, LANES), f32),
    pltpu.VMEM((HALF, LANES), f32),
    pltpu.VMEM((WIDE, LANES), f32),
]


def final_kernel(
    rows_first, sigma_first, held, pair_wide, weight_wide, rows_ref, sigma_ref,
    field, packed, spread, wide, half_sig, sig, rows_out, sigma_out, sems,
):
    copies = [
        pltpu.make_async_copy(rows_first, rows_ref.at[0, 0], sems.at[0]),
        pltpu.make_async_copy(sigma_first, sigma_ref.at[0, 0], sems.at[1]),
        pltpu.make_async_copy(rows_out, rows_ref.at[1, 0], sems.at[2]),
        pltpu.make_async_copy(sigma_out, sigma_ref.at[1, 0], sems.at[3]),
    ]
    copies[0].start()
    copies[1].start()
    rows_out[...] = held[...].T
    copies[2].start()
    tiles, collect = self_energy(held, None, pair_wide, weight_wide, field, packed, spread, wide, half_sig, sig)
    tiles(0, 8)
    collect(0, False)
    collect(1, False)
    sigma_out[...] = sig[...].T.astype(bf16)
    copies[3].start()
    for copy in copies:
        copy.wait()


def window_kernel(
    green_hbm, panel_hbm, inv_in, pair_wide, weight_wide,
    rows_ref, sigma_ref, last_ref,
    field, packed, spread, wide, half_sig, sig,
    green, panel_raw, panel_now, panel_next, inv_ref, held, sigma_out,
    sib_send, sib_recv, sums, msg_send, msg_recv, unit_send, unit_recv,
    load_sem, in_sem, inv_ss, inv_rs, sib_ss, sib_rs, msg_ss, msg_rs, unit_ss, unit_rs,
    st_ss, st_rs, st_ls, a1_ss, a1_rs, a2_ss, a2_rs, b1_ss, b1_rs, b2_ss, b2_rs,
):
    hist, tsec = lax.axis_index("hist"), lax.axis_index("tsec")
    chip, core = hist // 2, hist % 2
    z, y = tsec // 4, tsec % 4
    sibling = chip * 2 + 1 - core
    holder = core == y // 2
    depth = panel_now.shape[1]

    def at_chip(o, which):
        return ((chip + o) % 4) * 2 + which

    def loads(d):
        lanes = pl.ds(pl.multiple_of(d * LANES, LANES), LANES)
        return [
            pltpu.make_async_copy(
                green_hbm.at[part, :, lanes],
                green.at[d, :, pl.ds(part * LANES, LANES)],
                load_sem.at[d, part],
            )
            for part in range(2)
        ]

    panel_load = pltpu.make_async_copy(panel_hbm, panel_raw, in_sem.at[0])
    inv_keep = pltpu.make_async_copy(inv_in, inv_ref.at[core], in_sem.at[1])
    panel_load.start()
    for o in (2, 1, 3, 0):
        for d in (at_chip(o, 1 - core), at_chip(o, core)):
            for copy in loads(d):
                copy.start()
    inv_keep.start()

    barrier = pltpu.get_barrier_semaphore()

    def greet(h, t):
        pl.semaphore_signal(barrier, inc=1, device_id={"hist": h, "tsec": t}, device_id_type=MESH)

    greet(sibling, tsec)
    for o in range(1, 4):
        greet(at_chip(o, core), tsec)
        greet(hist, z * 4 + (y + o) % 4)
        greet(hist, ((z + o) % 4) * 4 + y)
    for h in range(8):
        @pl.when(jnp.logical_and(holder, jnp.logical_or(hist != h, z != chip)))
        def _():
            greet(h, chip * 4 + y)

    panel_load.wait()
    for r in range(depth // HALF):
        panel_now[:, r * HALF : (r + 1) * HALF] = panel_raw[r * HALF : (r + 1) * HALF, :].T
    own_part = hist == 2 * z + y // 2
    is_last = jnp.where(hist == 7, 1.0, 0.0).astype(f32)

    def remote(src, dst, ss, rs, h, t):
        return pltpu.make_async_remote_copy(
            src_ref=src, dst_ref=dst, send_sem=ss, recv_sem=rs,
            device_id={"hist": h, "tsec": t}, device_id_type=MESH,
        )

    inv_give = remote(inv_in, inv_ref.at[core], inv_ss, inv_rs, sibling, tsec)
    inv_take = remote(inv_in, inv_ref.at[1 - core], inv_ss, inv_rs, sibling, tsec)

    def memory(run):
        k = min(run, 1)
        count = WIDE if run == 0 else HALF
        half = count // 2
        base = HALF if run == 2 else 0
        upper, lower = pl.ds(base, half), pl.ds(base + half, half)
        whole, msg_rows = pl.ds(base, count), pl.ds(base // 2, half)

        def chunk(d):
            left = panel_now[...] if run == 0 else panel_next[base : base + count, :]
            out = dot(left, green[d])
            re = out[:half, :LANES] - out[half:, LANES:]
            im = out[half:, :LANES] + out[:half, LANES:]
            if k == 0:
                tail = green[d, green.shape[1] - HALF :, :].astype(f32) * is_last
                re, im = re + tail[:, :LANES], im + tail[:, LANES:]
            return re, im

        def swap(i):
            return remote(
                sib_send.at[k, i, whole], sib_recv.at[k, i, whole], sib_ss.at[run, i], sib_rs.at[run, i], sibling, tsec
            )

        def messages(o):
            there, n = at_chip(o, core), o - 1
            return (
                remote(msg_send.at[k, n, msg_rows], msg_recv.at[k, n, msg_rows], msg_ss.at[run, n], msg_rs.at[run, n], there, tsec),
                remote(unit_send.at[run, n], unit_recv.at[run, n], unit_ss.at[run, n], unit_rs.at[run, n], there, tsec),
            )

        def offset(i):
            return jnp.where(i == 0, 2, jnp.where(i == 1, 1, jnp.where(i == 2, 3, 0)))

        def finish(last):
            swap(last).wait()
            o = offset(last)
            re = sums[k, last, upper] + sib_recv[k, last, upper]
            im = sums[k, last, lower] + sib_recv[k, last, lower]
            peak = jnp.maximum(jnp.max(jnp.maximum(jnp.abs(re), jnp.abs(im))), 1e-30)
            scale = PEAK / peak
            high = jnp.round(re * scale).astype(i32)
            low = jnp.round(im * scale).astype(i32)
            msg_send[k, o - 1, msg_rows] = lax.shift_left(high, 16) | (low & 0xFFFF)
            unit_send[run, o - 1] = jnp.full((8, LANES), 1.0, f32) * (peak / PEAK)
            for copy in messages(o):
                copy.start()

        late = 1 if k == 0 else 0

        def step(i, carry):
            far = at_chip(offset(i), 1 - core)
            if k == 0:
                for copy in loads(far):
                    copy.wait()
            re, im = chunk(far)
            sib_send[k, i, upper] = re
            sib_send[k, i, lower] = im
            if k == 0:
                @pl.when(i == 1)
                def _():
                    pl.semaphore_wait(barrier, jnp.where(own_part, 13, 14))
                    swap(0).start()

                @pl.when(i >= 1)
                def _():
                    swap(i).start()

                @pl.when(i == 3)
                def _():
                    inv_give.start()
            else:
                swap(i).start()

            @pl.when(i > late)
            def _():
                finish(i - 1 - late)

            near = at_chip(offset(i), core)
            if k == 0:
                for copy in loads(near):
                    copy.wait()
            re, im = chunk(near)
            sums[k, i, upper] = re
            sums[k, i, lower] = im
            return carry

        lax.fori_loop(0, 4, step, 0)
        for last in range(3 - late, 3):
            finish(last)
        swap(3).wait()

        def collect():
            re = sums[k, 3, upper] + sib_recv[k, 3, upper]
            im = sums[k, 3, lower] + sib_recv[k, 3, lower]
            for o in (1, 3, 2):
                for copy in messages(o):
                    copy.wait()
                both = msg_recv[k, o - 1, msg_rows]
                unit = unit_recv[run, o - 1, :1, :1]
                re = re + lax.shift_right_arithmetic(both, 16).astype(f32) * unit
                im = im + lax.shift_right_arithmetic(lax.shift_left(both, 16), 16).astype(f32) * unit
            return re, im

        return collect

    def first(p, j):
        slot = pl.ds(pl.multiple_of((y % 2) * 1024 + hist * LANES, LANES), LANES)
        rows = pl.ds(p * HALF + j * 64, 64)
        return remote(
            sigma_out.at[rows], panel_next.at[rows, slot], st_ss.at[p, j], st_rs.at[p, hist], 2 * z + y // 2, 4 * j + y
        )

    def first_here(p, j):
        slot = pl.ds(pl.multiple_of((y % 2) * 1024 + hist * LANES, LANES), LANES)
        rows = pl.ds(p * HALF + j * 64, 64)
        return pltpu.make_async_copy(sigma_out.at[rows], panel_next.at[rows, slot], st_ls.at[p])

    def piece(p, second, j, odd):
        rows = pl.ds(pl.multiple_of(p * HALF + j * 64 + second * 32, 32), 32)
        return panel_next.at[rows, pl.ds(pl.multiple_of(odd * 1024, 1024), 1024)]

    def pass_on(p, second, j, odd, ss, rs, t):
        return remote(piece(p, second, j, odd), piece(p, second, j, odd), ss, rs, hist, t)

    def along_y(n):
        return z * 4 + (y + n) % 4

    def along_z(n):
        return ((z + n) % 4) * 4 + y

    def a1(p, n):
        return pass_on(p, 0, z, y % 2, a1_ss.at[p, n - 1], a1_rs.at[p, y % 2], along_y(n))

    def b1(p, n):
        return pass_on(p, 1, z, y % 2, b1_ss.at[p, n - 1], b1_rs.at[p, z], along_z(n))

    def a2(p, odd, n):
        return pass_on(p, 0, z, odd, a2_ss.at[p, odd, n - 1], a2_rs.at[p, z, odd], along_z(n))

    def b2(p, m, n):
        j = (z + m) % 4
        return pass_on(p, 1, j, y % 2, b2_ss.at[p, m, n - 1], b2_rs.at[p, j, y % 2], along_y(n))

    def exchange(p):
        for j in range(4):
            here = jnp.logical_and(own_part, z == j)

            @pl.when(jnp.logical_not(here))
            def _():
                first(p, j).start()

            @pl.when(here)
            def _():
                first_here(p, j).start()

    def arrived(p, second, j, odd, rs):
        pass_on(p, second, j, odd, a1_ss.at[p, 0], rs, along_y(1)).wait_recv()

    def relay_first(p):
        @pl.when(holder)
        def _():
            for h in range(8):
                slot = pl.ds(pl.multiple_of((y % 2) * 1024 + h * LANES, LANES), LANES)
                rows = pl.ds(pl.multiple_of(p * HALF + z * 64, 64), 64)

                @pl.when(jnp.logical_or(hist != h, z != chip))
                def _():
                    remote(
                        sigma_out.at[pl.ds(0, 64)], panel_next.at[rows, slot], st_ss.at[p, 0], st_rs.at[p, h], sibling, tsec
                    ).wait_recv()

            for j in range(4):
                @pl.when(jnp.logical_and(own_part, z == j))
                def _():
                    first_here(p, j).wait()

            for n in (2, 1, 3):
                a1(p, n).start()
                b1(p, n).start()
            for n in (2, 1, 3):
                a2(p, y % 2, n).start()
                b2(p, 0, n).start()

    def relay_second(p):
        for odd in range(2):
            @pl.when(2 * core + odd != y)
            def _():
                arrived(p, 0, z, odd, a1_rs.at[p, odd])
                for n in (2, 1, 3):
                    a2(p, odd, n).start()

        @pl.when(holder)
        def _():
            for m in (1, 3, 2):
                j = (z + m) % 4
                arrived(p, 1, j, y % 2, b1_rs.at[p, j])
                for n in (2, 1, 3):
                    b2(p, m, n).start()

    def settle(p):
        for odd in range(2):
            for m in (1, 3, 2):
                j = (z + m) % 4
                arrived(p, 0, j, odd, a2_rs.at[p, j, odd])

            @pl.when(2 * core + odd != y)
            def _():
                for j in range(4):
                    arrived(p, 1, j, odd, b2_rs.at[p, j, odd])

    def drain(p):
        for j in range(4):
            @pl.when(jnp.logical_not(jnp.logical_and(own_part, z == j)))
            def _():
                first(p, j).wait_send()
        for n in range(1, 4):
            for odd in range(2):
                a2(p, odd, n).wait_send()

        @pl.when(holder)
        def _():
            for n in range(1, 4):
                a1(p, n).wait_send()
                b1(p, n).wait_send()
                for m in range(4):
                    b2(p, m, n).wait_send()

    def solve(k, rhs):
        both = jnp.concatenate([rhs[:HALF], rhs[HALF:]], axis=1)
        high = both.astype(bf16)
        low = (both - high.astype(f32)).astype(bf16)
        out = dot(inv_ref[k], high)
        out = out[:WIDE] + out[WIDE:] + dot(inv_ref[k, :WIDE], low)
        held[:HALF] = out[:HALF, :LANES] - out[HALF:, LANES:]
        held[HALF:] = out[HALF:, :LANES] + out[:HALF, LANES:]

    re, im = memory(0)()
    inv_keep.wait()
    inv_take.wait_recv()
    solve(0, jnp.concatenate([re, im], axis=0))
    tiles, collect = self_energy(
        held, sigma_out, pair_wide, weight_wide, field, packed, spread, wide, half_sig, sig
    )
    tiles(0, 4)
    collect(0, True)
    exchange(0)
    tiles(4, 6)
    relay_first(0)
    tiles(6, 8)
    collect(1, True)
    exchange(1)
    relay_second(0)
    rows_ref[...] = held[...].T
    sigma_ref[...] = sig[...].T.astype(bf16)
    relay_first(1)
    relay_second(1)
    settle(0)
    results = [memory(1)]
    settle(1)
    results.append(memory(2))
    for p in range(2):
        re, im = results[p]()
        for n in range(8):
            for part, value in enumerate((re, im)):
                at = part * HALF + n * N + p * 16
                held[at : at + 16] = held[at : at + 16] + value[n * 16 : n * 16 + 16]
    solve(1, held[...])
    last_ref[...] = held[...]
    inv_give.wait_send()
    for p in range(2):
        drain(p)


def per_device(hist_green, sigma_panel, step_operator, coupling, pair_index):
    inverse, pairs, weights = prepare(step_operator, pair_index.reshape(3 * Q, PAIRS), coupling)
    depth = sigma_panel.shape[0]
    anywhere = pl.BlockSpec(memory_space=pl.ANY)
    vmem = pl.BlockSpec(memory_space=pltpu.VMEM)
    dma = pltpu.SemaphoreType.DMA
    rows_first, sigma_first, last = pl.pallas_call(
        window_kernel,
        out_shape=(
            jax.ShapeDtypeStruct((LANES, WIDE), f32),
            jax.ShapeDtypeStruct((LANES, WIDE), bf16),
            jax.ShapeDtypeStruct((WIDE, LANES), f32),
        ),
        in_specs=[anywhere, anywhere, vmem, vmem, vmem],
        out_specs=(vmem, vmem, vmem),
        scratch_shapes=ENERGY_SCRATCH + [
            pltpu.VMEM((8, depth, 2 * LANES), bf16),
            pltpu.VMEM((depth, WIDE), bf16),
            pltpu.VMEM((WIDE, depth), bf16),
            pltpu.VMEM((WIDE, depth), bf16),
            pltpu.VMEM((NBLK, 2 * WIDE, HALF), bf16),
            pltpu.VMEM((WIDE, LANES), f32),
            pltpu.VMEM((WIDE, LANES), bf16),
            pltpu.VMEM((NBLK, 4, WIDE, LANES), f32),
            pltpu.VMEM((NBLK, 4, WIDE, LANES), f32),
            pltpu.VMEM((NBLK, 4, WIDE, LANES), f32),
            pltpu.VMEM((NBLK, 3, HALF, LANES), i32),
            pltpu.VMEM((NBLK, 3, HALF, LANES), i32),
            pltpu.VMEM((3, 3, 8, LANES), f32),
            pltpu.VMEM((3, 3, 8, LANES), f32),
            dma((8, 2)), dma((2,)), dma(()), dma(()),
            dma((3, 4)), dma((3, 4)),
            dma((3, 3)), dma((3, 3)),
            dma((3, 3)), dma((3, 3)),
            dma((2, 4)), dma((2, 8)), dma((2,)),
            dma((2, 3)), dma((2, 2)), dma((2, 2, 3)), dma((2, 4, 2)),
            dma((2, 3)), dma((2, 4)), dma((2, 4, 3)), dma((2, 4, 2)),
        ],
        compiler_params=pltpu.CompilerParams(
            collective_id=0, has_side_effects=True, vmem_limit_bytes=50 << 20
        ),
    )(hist_green, sigma_panel, inverse, pairs, weights)
    return pl.pallas_call(
        final_kernel,
        out_shape=(
            jax.ShapeDtypeStruct((NBLK, 1, LANES, WIDE), f32),
            jax.ShapeDtypeStruct((NBLK, 1, LANES, WIDE), bf16),
        ),
        in_specs=[anywhere, anywhere, vmem, vmem, vmem],
        out_specs=(anywhere, anywhere),
        scratch_shapes=ENERGY_SCRATCH + [
            pltpu.VMEM((LANES, WIDE), f32),
            pltpu.VMEM((LANES, WIDE), bf16),
            dma((4,)),
        ],
        compiler_params=pltpu.CompilerParams(vmem_limit_bytes=24 << 20),
    )(rows_first, sigma_first, last, pairs, weights)


def solution(mesh):
    return jax.shard_map(
        per_device,
        mesh=mesh,
        in_specs=(P(None, "hist", "tsec"), P("hist", None), P(), P(), P()),
        out_specs=(P(None, "tsec", "hist", None), P(None, "tsec", "hist", None)),
        check_vma=False,
    )
```

```python
import functools

import jax
import jax.numpy as jnp
from jax import lax
from jax.experimental import pallas as pl
from jax.experimental.pallas import tpu as pltpu
from jax.sharding import PartitionSpec as P

N = 32
B = 8
NBLK = 2
Q = 8
HALF = B * N
WIDE = 2 * HALF
LANES = 128
PAIRS = N * N
TILES = PAIRS // LANES
MESH = pl.DeviceIdType.MESH
f32, bf16, i32 = jnp.float32, jnp.bfloat16, jnp.int32
HIGHEST = lax.Precision.HIGHEST
PEAK = 32000.0


def dot(left, right, precision=None):
    return jnp.dot(left, right, preferred_element_type=f32, precision=precision)


def prepare_kernel(op_ref, pair_ref, weight_ref, out_ref, pair_wide, weight_wide, x_ref, r_ref):
    a_ref = op_ref.at[lax.axis_index("hist") % 2]
    rows = lax.broadcasted_iota(i32, (HALF, HALF), 0)
    cols = lax.broadcasted_iota(i32, (HALF, HALF), 1)
    eye = jnp.where(rows == cols, 1.0, 0.0).astype(f32)
    ar, ai = a_ref[0], a_ref[1]
    inv_row = 1.0 / jnp.sum(ar * eye, axis=0, keepdims=True)
    inv_col = 1.0 / jnp.sum(ar * eye, axis=1, keepdims=True)
    x_ref[:, :HALF] = inv_col * (eye + (eye - ar * inv_row))
    x_ref[:, HALF:] = inv_col * (-ai * inv_row)

    def product(left, right, precision):
        out = dot(left, right, precision)
        return out[:HALF, :HALF] - out[HALF:, HALF:], out[:HALF, HALF:] + out[HALF:, :HALF]

    def residual():
        re, im = product(a_ref[...].reshape(WIDE, HALF), x_ref[...], HIGHEST)
        re, im = eye - re, -im
        r_ref[:, :HALF] = re
        r_ref[:, HALF:] = im
        return jnp.max(jnp.sum(jnp.abs(re) + jnp.abs(im), axis=0, keepdims=True))

    def improve(precision):
        left = jnp.concatenate([x_ref[:, :HALF], x_ref[:, HALF:]], axis=0)
        re, im = product(left, r_ref[...], precision)
        x_ref[:, :HALF] = x_ref[:, :HALF] + re
        x_ref[:, HALF:] = x_ref[:, HALF:] + im

    def unfinished(carry):
        step, norm = carry
        return jnp.logical_and(step < 40, norm > 3e-3)

    def again(carry):
        improve(HIGHEST)
        return carry[0] + 1, residual()

    lax.while_loop(unfinished, again, (jnp.int32(0), residual()))
    improve(None)
    for part in range(2):
        value = x_ref[:, part * HALF : (part + 1) * HALF]
        high = value.astype(bf16)
        out_ref[part * HALF : (part + 1) * HALF] = high
        out_ref[WIDE + part * HALF : WIDE + (part + 1) * HALF] = (value - high.astype(f32)).astype(bf16)
    for j in range(TILES):
        lanes = slice(j * LANES, (j + 1) * LANES)
        for r in range(3 * Q):
            pair_wide[j, r] = jnp.broadcast_to(pair_ref[r : r + 1, lanes], (8, LANES))
        for r in range(Q):
            weight_wide[j, r] = jnp.broadcast_to(weight_ref[r : r + 1, lanes], (8, LANES))


def prepare(step_operator, pairs, coupling):
    vmem = pl.BlockSpec(memory_space=pltpu.VMEM)
    return pl.pallas_call(
        prepare_kernel,
        out_shape=(
            jax.ShapeDtypeStruct((2 * WIDE, HALF), bf16),
            jax.ShapeDtypeStruct((TILES, 3 * Q, 8, LANES), i32),
            jax.ShapeDtypeStruct((TILES, Q, 8, LANES), f32),
        ),
        in_specs=[vmem] * 3,
        out_specs=(vmem,) * 3,
        scratch_shapes=[pltpu.VMEM((HALF, WIDE), f32), pltpu.VMEM((HALF, WIDE), f32)],
        compiler_params=pltpu.CompilerParams(vmem_limit_bytes=32 << 20),
    )(step_operator, pairs, coupling)


def regroup(count, pick, store):
    lane_group = lax.broadcasted_iota(i32, (count, LANES), 1) // N
    for s in range(4):
        value = None
        for a in range(4):
            moved = pick(a)
            if a != s:
                moved = pltpu.roll(moved, (N * (a - s)) % LANES, 1)
            value = moved if value is None else jnp.where(lane_group == a, moved, value)
        store(s, value)


def self_energy(held, sigma_out, pair_wide, weight_wide, field, packed, spread, wide, half_sig, sig):
    peak = jnp.maximum(jnp.max(jnp.abs(held[...])), 1e-30)
    scale, unit = PEAK / peak, peak / PEAK

    def store_field(s, value):
        whole = jnp.round(value * scale).astype(i32)
        both = lax.shift_left(whole[:64], 16) | (whole[64:] & 0xFFFF)
        field[s] = both
    regroup(LANES, lambda a: held[pl.ds(a, LANES, stride=4), :], store_field)
    for j in range(TILES):
        for s in range(4):
            packed[j, s] = field[s, pl.ds(j, 8, stride=TILES), :]

    def tile(j, carry):
        def term(q, acc):
            values = []
            for f in range(3):
                pair = pair_wide[j, f * Q + q]
                low, high = pair & (LANES - 1), lax.shift_right_logical(pair, 7)
                masks = [high == n for n in range(1, TILES)]
                parts = []
                for s in range(4):
                    found = jnp.take_along_axis(packed[0, s], low, axis=1)
                    for n in range(1, TILES):
                        found = jnp.where(masks[n - 1], jnp.take_along_axis(packed[n, s], low, axis=1), found)
                    parts.append((
                        lax.shift_right_arithmetic(found, 16).astype(f32),
                        lax.shift_right_arithmetic(lax.shift_left(found, 16), 16).astype(f32),
                    ))
                values.append(parts)
            weight = weight_wide[j, q]
            result = []
            for s in range(4):
                (ar, ai), (br, bi), (cr, ci) = values[0][s], values[1][s], values[2][s]
                pr, pi = ar * br - ai * bi, ar * bi + ai * br
                result.append(acc[2 * s] + weight * (pr * cr + pi * ci))
                result.append(acc[2 * s + 1] + weight * (pi * cr - pr * ci))
            return tuple(result)

        acc = lax.fori_loop(0, Q, term, tuple(jnp.zeros((8, LANES), f32) for _ in range(8)), unroll=8)
        for s in range(4):
            for part in range(2):
                spread[s, j, part * 8 : part * 8 + 8, :] = acc[2 * s + part] * (unit * unit * unit)
        return carry

    def tiles(start, stop):
        lax.fori_loop(start, stop, tile, 0)

    def store_piece(a, value):
        half_sig[pl.ds(a, 64, stride=4), :] = value

    def collect(p, share):
        for s in range(4):
            for jj in range(4):
                for part in range(2):
                    wide[s, pl.ds(part * 32 + jj, 8, stride=4), :] = spread[s, p * 4 + jj, part * 8 : part * 8 + 8, :]
        regroup(64, lambda s: wide[s], store_piece)
        if share:
            sigma_out[p * HALF : (p + 1) * HALF] = half_sig[...].astype(bf16)
        for n in range(16):
            sig[n * N + p * 16 : n * N + p * 16 + 16] = half_sig[n * 16 : n * 16 + 16]

    return tiles, collect


ENERGY_SCRATCH = [
    pltpu.VMEM((4, 64, LANES), i32),
    pltpu.VMEM((TILES, 4, 8, LANES), i32),
    pltpu.VMEM((4, TILES, 16, LANES), f32),
    pltpu.VMEM((4, 64, LANES), f32),
    pltpu.VMEM((HALF, LANES), f32),
    pltpu.VMEM((WIDE, LANES), f32),
]


def final_kernel(
    rows_first, sigma_first, held, pair_wide, weight_wide, rows_ref, sigma_ref,
    field, packed, spread, wide, half_sig, sig, rows_out, sigma_out, sems,
):
    copies = [
        pltpu.make_async_copy(rows_first, rows_ref.at[0, 0], sems.at[0]),
        pltpu.make_async_copy(sigma_first, sigma_ref.at[0, 0], sems.at[1]),
        pltpu.make_async_copy(rows_out, rows_ref.at[1, 0], sems.at[2]),
        pltpu.make_async_copy(sigma_out, sigma_ref.at[1, 0], sems.at[3]),
    ]
    copies[0].start()
    copies[1].start()
    rows_out[...] = held[...].T
    copies[2].start()
    tiles, collect = self_energy(held, None, pair_wide, weight_wide, field, packed, spread, wide, half_sig, sig)
    tiles(0, 8)
    collect(0, False)
    collect(1, False)
    sigma_out[...] = sig[...].T.astype(bf16)
    copies[3].start()
    for copy in copies:
        copy.wait()


def window_kernel(
    green_hbm, panel_hbm, inv_in, pair_wide, weight_wide,
    rows_ref, sigma_ref, last_ref,
    field, packed, spread, wide, half_sig, sig,
    green, panel_raw, panel_now, panel_next, inv_ref, held, sigma_out,
    sib_send, sib_recv, sums, msg_send, msg_recv, unit_send, unit_recv,
    load_sem, in_sem, inv_ss, inv_rs, sib_ss, sib_rs, msg_ss, msg_rs, unit_ss, unit_rs,
    st_ss, st_rs, st_ls, a1_ss, a1_rs, a2_ss, a2_rs, b1_ss, b1_rs, b2_ss, b2_rs,
):
    hist, tsec = lax.axis_index("hist"), lax.axis_index("tsec")
    chip, core = hist // 2, hist % 2
    z, y = tsec // 4, tsec % 4
    sibling = chip * 2 + 1 - core
    holder = core == y // 2
    depth = panel_now.shape[1]

    def at_chip(o, which):
        return ((chip + o) % 4) * 2 + which

    def loads(d):
        lanes = pl.ds(pl.multiple_of(d * LANES, LANES), LANES)
        return [
            pltpu.make_async_copy(
                green_hbm.at[part, :, lanes],
                green.at[d, :, pl.ds(part * LANES, LANES)],
                load_sem.at[d, part],
            )
            for part in range(2)
        ]

    panel_load = pltpu.make_async_copy(panel_hbm, panel_raw, in_sem.at[0])
    inv_keep = pltpu.make_async_copy(inv_in, inv_ref.at[core], in_sem.at[1])
    panel_load.start()
    for o in (2, 1, 3, 0):
        for d in (at_chip(o, 1 - core), at_chip(o, core)):
            for copy in loads(d):
                copy.start()
    inv_keep.start()

    barrier = pltpu.get_barrier_semaphore()

    def greet(h, t):
        pl.semaphore_signal(barrier, inc=1, device_id={"hist": h, "tsec": t}, device_id_type=MESH)

    greet(sibling, tsec)
    for o in range(1, 4):
        greet(at_chip(o, core), tsec)
        greet(hist, z * 4 + (y + o) % 4)
        greet(hist, ((z + o) % 4) * 4 + y)
    for h in range(8):
        @pl.when(jnp.logical_and(holder, jnp.logical_or(hist != h, z != chip)))
        def _():
            greet(h, chip * 4 + y)

    panel_load.wait()
    for r in range(depth // HALF):
        panel_now[:, r * HALF : (r + 1) * HALF] = panel_raw[r * HALF : (r + 1) * HALF, :].T
    own_part = hist == 2 * z + y // 2
    is_last = jnp.where(hist == 7, 1.0, 0.0).astype(f32)

    def remote(src, dst, ss, rs, h, t):
        return pltpu.make_async_remote_copy(
            src_ref=src, dst_ref=dst, send_sem=ss, recv_sem=rs,
            device_id={"hist": h, "tsec": t}, device_id_type=MESH,
        )

    inv_give = remote(inv_in, inv_ref.at[core], inv_ss, inv_rs, sibling, tsec)
    inv_take = remote(inv_in, inv_ref.at[1 - core], inv_ss, inv_rs, sibling, tsec)

    def memory(run):
        k = min(run, 1)
        count = WIDE if run == 0 else HALF
        half = count // 2
        base = HALF if run == 2 else 0
        upper, lower = pl.ds(base, half), pl.ds(base + half, half)
        whole, msg_rows = pl.ds(base, count), pl.ds(base // 2, half)

        def chunk(d):
            left = panel_now[...] if run == 0 else panel_next[base : base + count, :]
            out = dot(left, green[d])
            re = out[:half, :LANES] - out[half:, LANES:]
            im = out[half:, :LANES] + out[:half, LANES:]
            if k == 0:
                tail = green[d, green.shape[1] - HALF :, :].astype(f32) * is_last
                re, im = re + tail[:, :LANES], im + tail[:, LANES:]
            return re, im

        def swap(i):
            return remote(
                sib_send.at[k, i, whole], sib_recv.at[k, i, whole], sib_ss.at[run, i], sib_rs.at[run, i], sibling, tsec
            )

        def messages(o):
            there, n = at_chip(o, core), o - 1
            return (
                remote(msg_send.at[k, n, msg_rows], msg_recv.at[k, n, msg_rows], msg_ss.at[run, n], msg_rs.at[run, n], there, tsec),
                remote(unit_send.at[run, n], unit_recv.at[run, n], unit_ss.at[run, n], unit_rs.at[run, n], there, tsec),
            )

        def offset(i):
            return jnp.where(i == 0, 2, jnp.where(i == 1, 1, jnp.where(i == 2, 3, 0)))

        def finish(last):
            swap(last).wait()
            o = offset(last)
            re = sums[k, last, upper] + sib_recv[k, last, upper]
            im = sums[k, last, lower] + sib_recv[k, last, lower]
            peak = jnp.maximum(jnp.max(jnp.maximum(jnp.abs(re), jnp.abs(im))), 1e-30)
            scale = PEAK / peak
            high = jnp.round(re * scale).astype(i32)
            low = jnp.round(im * scale).astype(i32)
            msg_send[k, o - 1, msg_rows] = lax.shift_left(high, 16) | (low & 0xFFFF)
            unit_send[run, o - 1] = jnp.full((8, LANES), 1.0, f32) * (peak / PEAK)
            for copy in messages(o):
                copy.start()

        late = 0

        def step(i, carry):
            far = at_chip(offset(i), 1 - core)
            if k == 0:
                for copy in loads(far):
                    copy.wait()
            re, im = chunk(far)
            sib_send[k, i, upper] = re
            sib_send[k, i, lower] = im
            if k == 0:
                @pl.when(i == 0)
                def _():
                    pl.semaphore_wait(barrier, jnp.where(own_part, 13, 14))

                swap(i).start()

                @pl.when(i == 3)
                def _():
                    inv_give.start()
            else:
                swap(i).start()

            @pl.when(i > late)
            def _():
                finish(i - 1 - late)

            near = at_chip(offset(i), core)
            if k == 0:
                for copy in loads(near):
                    copy.wait()
            re, im = chunk(near)
            sums[k, i, upper] = re
            sums[k, i, lower] = im
            return carry

        lax.fori_loop(0, 4, step, 0)
        for last in range(3 - late, 3):
            finish(last)
        swap(3).wait()

        def collect():
            re = sums[k, 3, upper] + sib_recv[k, 3, upper]
            im = sums[k, 3, lower] + sib_recv[k, 3, lower]
            for o in (1, 3, 2):
                for copy in messages(o):
                    copy.wait()
                both = msg_recv[k, o - 1, msg_rows]
                unit = unit_recv[run, o - 1, :1, :1]
                re = re + lax.shift_right_arithmetic(both, 16).astype(f32) * unit
                im = im + lax.shift_right_arithmetic(lax.shift_left(both, 16), 16).astype(f32) * unit
            return re, im

        return collect

    def first(p, j):
        slot = pl.ds(pl.multiple_of((y % 2) * 1024 + hist * LANES, LANES), LANES)
        rows = pl.ds(p * HALF + j * 64, 64)
        return remote(
            sigma_out.at[rows], panel_next.at[rows, slot], st_ss.at[p, j], st_rs.at[p, hist], 2 * z + y // 2, 4 * j + y
        )

    def first_here(p, j):
        slot = pl.ds(pl.multiple_of((y % 2) * 1024 + hist * LANES, LANES), LANES)
        rows = pl.ds(p * HALF + j * 64, 64)
        return pltpu.make_async_copy(sigma_out.at[rows], panel_next.at[rows, slot], st_ls.at[p])

    def piece(p, second, j, odd):
        rows = pl.ds(pl.multiple_of(p * HALF + j * 64 + second * 32, 32), 32)
        return panel_next.at[rows, pl.ds(pl.multiple_of(odd * 1024, 1024), 1024)]

    def pass_on(p, second, j, odd, ss, rs, t):
        return remote(piece(p, second, j, odd), piece(p, second, j, odd), ss, rs, hist, t)

    def along_y(n):
        return z * 4 + (y + n) % 4

    def along_z(n):
        return ((z + n) % 4) * 4 + y

    def a1(p, n):
        return pass_on(p, 0, z, y % 2, a1_ss.at[p, n - 1], a1_rs.at[p, y % 2], along_y(n))

    def b1(p, n):
        return pass_on(p, 1, z, y % 2, b1_ss.at[p, n - 1], b1_rs.at[p, z], along_z(n))

    def a2(p, odd, n):
        return pass_on(p, 0, z, odd, a2_ss.at[p, odd, n - 1], a2_rs.at[p, z, odd], along_z(n))

    def b2(p, m, n):
        j = (z + m) % 4
        return pass_on(p, 1, j, y % 2, b2_ss.at[p, m, n - 1], b2_rs.at[p, j, y % 2], along_y(n))

    def exchange(p):
        for j in range(4):
            here = jnp.logical_and(own_part, z == j)

            @pl.when(jnp.logical_not(here))
            def _():
                first(p, j).start()

            @pl.when(here)
            def _():
                first_here(p, j).start()

    def arrived(p, second, j, odd, rs):
        pass_on(p, second, j, odd, a1_ss.at[p, 0], rs, along_y(1)).wait_recv()

    def relay_first(p):
        @pl.when(holder)
        def _():
            for h in range(8):
                slot = pl.ds(pl.multiple_of((y % 2) * 1024 + h * LANES, LANES), LANES)
                rows = pl.ds(pl.multiple_of(p * HALF + z * 64, 64), 64)

                @pl.when(jnp.logical_or(hist != h, z != chip))
                def _():
                    remote(
                        sigma_out.at[pl.ds(0, 64)], panel_next.at[rows, slot], st_ss.at[p, 0], st_rs.at[p, h], sibling, tsec
                    ).wait_recv()

            for j in range(4):
                @pl.when(jnp.logical_and(own_part, z == j))
                def _():
                    first_here(p, j).wait()

            for n in (2, 1, 3):
                a1(p, n).start()
                b1(p, n).start()
            for n in (2, 1, 3):
                a2(p, y % 2, n).start()
                b2(p, 0, n).start()

    def relay_second(p):
        for odd in range(2):
            @pl.when(2 * core + odd != y)
            def _():
                arrived(p, 0, z, odd, a1_rs.at[p, odd])
                for n in (2, 1, 3):
                    a2(p, odd, n).start()

        @pl.when(holder)
        def _():
            for m in (1, 3, 2):
                j = (z + m) % 4
                arrived(p, 1, j, y % 2, b1_rs.at[p, j])
                for n in (2, 1, 3):
                    b2(p, m, n).start()

    def settle(p):
        for odd in range(2):
            for m in (1, 3, 2):
                j = (z + m) % 4
                arrived(p, 0, j, odd, a2_rs.at[p, j, odd])

            @pl.when(2 * core + odd != y)
            def _():
                for j in range(4):
                    arrived(p, 1, j, odd, b2_rs.at[p, j, odd])

    def drain(p):
        for j in range(4):
            @pl.when(jnp.logical_not(jnp.logical_and(own_part, z == j)))
            def _():
                first(p, j).wait_send()
        for n in range(1, 4):
            for odd in range(2):
                a2(p, odd, n).wait_send()

        @pl.when(holder)
        def _():
            for n in range(1, 4):
                a1(p, n).wait_send()
                b1(p, n).wait_send()
                for m in range(4):
                    b2(p, m, n).wait_send()

    def solve(k, rhs):
        both = jnp.concatenate([rhs[:HALF], rhs[HALF:]], axis=1)
        high = both.astype(bf16)
        low = (both - high.astype(f32)).astype(bf16)
        out = dot(inv_ref[k], high)
        out = out[:WIDE] + out[WIDE:] + dot(inv_ref[k, :WIDE], low)
        held[:HALF] = out[:HALF, :LANES] - out[HALF:, LANES:]
        held[HALF:] = out[HALF:, :LANES] + out[:HALF, LANES:]

    re, im = memory(0)()
    inv_keep.wait()
    inv_take.wait_recv()
    solve(0, jnp.concatenate([re, im], axis=0))
    tiles, collect = self_energy(
        held, sigma_out, pair_wide, weight_wide, field, packed, spread, wide, half_sig, sig
    )
    tiles(0, 4)
    collect(0, True)
    exchange(0)
    tiles(4, 6)
    relay_first(0)
    tiles(6, 8)
    collect(1, True)
    exchange(1)
    relay_second(0)
    rows_ref[...] = held[...].T
    sigma_ref[...] = sig[...].T.astype(bf16)
    relay_first(1)
    relay_second(1)
    settle(0)
    results = [memory(1)]
    settle(1)
    results.append(memory(2))
    for p in range(2):
        re, im = results[p]()
        for n in range(8):
            for part, value in enumerate((re, im)):
                at = part * HALF + n * N + p * 16
                held[at : at + 16] = held[at : at + 16] + value[n * 16 : n * 16 + 16]
    solve(1, held[...])
    last_ref[...] = held[...]
    inv_give.wait_send()
    for p in range(2):
        drain(p)


def per_device(hist_green, sigma_panel, step_operator, coupling, pair_index):
    inverse, pairs, weights = prepare(step_operator, pair_index.reshape(3 * Q, PAIRS), coupling)
    depth = sigma_panel.shape[0]
    anywhere = pl.BlockSpec(memory_space=pl.ANY)
    vmem = pl.BlockSpec(memory_space=pltpu.VMEM)
    dma = pltpu.SemaphoreType.DMA
    rows_first, sigma_first, last = pl.pallas_call(
        window_kernel,
        out_shape=(
            jax.ShapeDtypeStruct((LANES, WIDE), f32),
            jax.ShapeDtypeStruct((LANES, WIDE), bf16),
            jax.ShapeDtypeStruct((WIDE, LANES), f32),
        ),
        in_specs=[anywhere, anywhere, vmem, vmem, vmem],
        out_specs=(vmem, vmem, vmem),
        scratch_shapes=ENERGY_SCRATCH + [
            pltpu.VMEM((8, depth, 2 * LANES), bf16),
            pltpu.VMEM((depth, WIDE), bf16),
            pltpu.VMEM((WIDE, depth), bf16),
            pltpu.VMEM((WIDE, depth), bf16),
            pltpu.VMEM((NBLK, 2 * WIDE, HALF), bf16),
            pltpu.VMEM((WIDE, LANES), f32),
            pltpu.VMEM((WIDE, LANES), bf16),
            pltpu.VMEM((NBLK, 4, WIDE, LANES), f32),
            pltpu.VMEM((NBLK, 4, WIDE, LANES), f32),
            pltpu.VMEM((NBLK, 4, WIDE, LANES), f32),
            pltpu.VMEM((NBLK, 3, HALF, LANES), i32),
            pltpu.VMEM((NBLK, 3, HALF, LANES), i32),
            pltpu.VMEM((3, 3, 8, LANES), f32),
            pltpu.VMEM((3, 3, 8, LANES), f32),
            dma((8, 2)), dma((2,)), dma(()), dma(()),
            dma((3, 4)), dma((3, 4)),
            dma((3, 3)), dma((3, 3)),
            dma((3, 3)), dma((3, 3)),
            dma((2, 4)), dma((2, 8)), dma((2,)),
            dma((2, 3)), dma((2, 2)), dma((2, 2, 3)), dma((2, 4, 2)),
            dma((2, 3)), dma((2, 4)), dma((2, 4, 3)), dma((2, 4, 2)),
        ],
        compiler_params=pltpu.CompilerParams(
            collective_id=0, has_side_effects=True, vmem_limit_bytes=50 << 20
        ),
    )(hist_green, sigma_panel, inverse, pairs, weights)
    return pl.pallas_call(
        final_kernel,
        out_shape=(
            jax.ShapeDtypeStruct((NBLK, 1, LANES, WIDE), f32),
            jax.ShapeDtypeStruct((NBLK, 1, LANES, WIDE), bf16),
        ),
        in_specs=[anywhere, anywhere, vmem, vmem, vmem],
        out_specs=(anywhere, anywhere),
        scratch_shapes=ENERGY_SCRATCH + [
            pltpu.VMEM((LANES, WIDE), f32),
            pltpu.VMEM((LANES, WIDE), bf16),
            dma((4,)),
        ],
        compiler_params=pltpu.CompilerParams(vmem_limit_bytes=24 << 20),
    )(rows_first, sigma_first, last, pairs, weights)


def solution(mesh):
    return jax.shard_map(
        per_device,
        mesh=mesh,
        in_specs=(P(None, "hist", "tsec"), P("hist", None), P(), P(), P()),
        out_specs=(P(None, "tsec", "hist", None), P(None, "tsec", "hist", None)),
        check_vma=False,
    )
```

```python
import functools

import jax
import jax.numpy as jnp
from jax import lax
from jax.experimental import pallas as pl
from jax.experimental.pallas import tpu as pltpu
from jax.sharding import PartitionSpec as P

N = 32
B = 8
NBLK = 2
Q = 8
HALF = B * N
WIDE = 2 * HALF
LANES = 128
PAIRS = N * N
TILES = PAIRS // LANES
MESH = pl.DeviceIdType.MESH
f32, bf16, i32 = jnp.float32, jnp.bfloat16, jnp.int32
HIGHEST = lax.Precision.HIGHEST
PEAK = 32000.0


def dot(left, right, precision=None):
    return jnp.dot(left, right, preferred_element_type=f32, precision=precision)


def prepare_kernel(op_ref, pair_ref, weight_ref, out_ref, pair_wide, weight_wide, x_ref, r_ref):
    a_ref = op_ref.at[lax.axis_index("hist") % 2]
    rows = lax.broadcasted_iota(i32, (HALF, HALF), 0)
    cols = lax.broadcasted_iota(i32, (HALF, HALF), 1)
    eye = jnp.where(rows == cols, 1.0, 0.0).astype(f32)
    ar, ai = a_ref[0], a_ref[1]
    inv_row = 1.0 / jnp.sum(ar * eye, axis=0, keepdims=True)
    inv_col = 1.0 / jnp.sum(ar * eye, axis=1, keepdims=True)
    x_ref[:, :HALF] = inv_col * (eye + (eye - ar * inv_row))
    x_ref[:, HALF:] = inv_col * (-ai * inv_row)

    def product(left, right, precision):
        out = dot(left, right, precision)
        return out[:HALF, :HALF] - out[HALF:, HALF:], out[:HALF, HALF:] + out[HALF:, :HALF]

    def residual():
        re, im = product(a_ref[...].reshape(WIDE, HALF), x_ref[...], HIGHEST)
        re, im = eye - re, -im
        r_ref[:, :HALF] = re
        r_ref[:, HALF:] = im
        return jnp.max(jnp.sum(jnp.abs(re) + jnp.abs(im), axis=0, keepdims=True))

    def improve(precision):
        left = jnp.concatenate([x_ref[:, :HALF], x_ref[:, HALF:]], axis=0)
        re, im = product(left, r_ref[...], precision)
        x_ref[:, :HALF] = x_ref[:, :HALF] + re
        x_ref[:, HALF:] = x_ref[:, HALF:] + im

    def unfinished(carry):
        step, norm = carry
        return jnp.logical_and(step < 40, norm > 3e-3)

    def again(carry):
        improve(HIGHEST)
        return carry[0] + 1, residual()

    lax.while_loop(unfinished, again, (jnp.int32(0), residual()))
    improve(None)
    for part in range(2):
        value = x_ref[:, part * HALF : (part + 1) * HALF]
        high = value.astype(bf16)
        out_ref[part * HALF : (part + 1) * HALF] = high
        out_ref[WIDE + part * HALF : WIDE + (part + 1) * HALF] = (value - high.astype(f32)).astype(bf16)
    for j in range(TILES):
        lanes = slice(j * LANES, (j + 1) * LANES)
        for r in range(3 * Q):
            pair_wide[j, r] = jnp.broadcast_to(pair_ref[r : r + 1, lanes], (8, LANES))
        for r in range(Q):
            weight_wide[j, r] = jnp.broadcast_to(weight_ref[r : r + 1, lanes], (8, LANES))


def prepare(step_operator, pairs, coupling):
    vmem = pl.BlockSpec(memory_space=pltpu.VMEM)
    return pl.pallas_call(
        prepare_kernel,
        out_shape=(
            jax.ShapeDtypeStruct((2 * WIDE, HALF), bf16),
            jax.ShapeDtypeStruct((TILES, 3 * Q, 8, LANES), i32),
            jax.ShapeDtypeStruct((TILES, Q, 8, LANES), f32),
        ),
        in_specs=[vmem] * 3,
        out_specs=(vmem,) * 3,
        scratch_shapes=[pltpu.VMEM((HALF, WIDE), f32), pltpu.VMEM((HALF, WIDE), f32)],
        compiler_params=pltpu.CompilerParams(vmem_limit_bytes=32 << 20),
    )(step_operator, pairs, coupling)


def regroup(count, pick, store):
    lane_group = lax.broadcasted_iota(i32, (count, LANES), 1) // N
    for s in range(4):
        value = None
        for a in range(4):
            moved = pick(a)
            if a != s:
                moved = pltpu.roll(moved, (N * (a - s)) % LANES, 1)
            value = moved if value is None else jnp.where(lane_group == a, moved, value)
        store(s, value)


def self_energy(held, sigma_out, pair_wide, weight_wide, field, packed, spread, wide, half_sig, sig):
    peak = jnp.maximum(jnp.max(jnp.abs(held[...])), 1e-30)
    scale, unit = PEAK / peak, peak / PEAK

    def store_field(s, value):
        whole = jnp.round(value * scale).astype(i32)
        both = lax.shift_left(whole[:64], 16) | (whole[64:] & 0xFFFF)
        field[s] = both
    regroup(LANES, lambda a: held[pl.ds(a, LANES, stride=4), :], store_field)
    for j in range(TILES):
        for s in range(4):
            packed[j, s] = field[s, pl.ds(j, 8, stride=TILES), :]

    def tile(j, carry):
        def term(q, acc):
            values = []
            for f in range(3):
                pair = pair_wide[j, f * Q + q]
                low, high = pair & (LANES - 1), lax.shift_right_logical(pair, 7)
                masks = [high == n for n in range(1, TILES)]
                parts = []
                for s in range(4):
                    found = jnp.take_along_axis(packed[0, s], low, axis=1)
                    for n in range(1, TILES):
                        found = jnp.where(masks[n - 1], jnp.take_along_axis(packed[n, s], low, axis=1), found)
                    parts.append((
                        lax.shift_right_arithmetic(found, 16).astype(f32),
                        lax.shift_right_arithmetic(lax.shift_left(found, 16), 16).astype(f32),
                    ))
                values.append(parts)
            weight = weight_wide[j, q]
            result = []
            for s in range(4):
                (ar, ai), (br, bi), (cr, ci) = values[0][s], values[1][s], values[2][s]
                pr, pi = ar * br - ai * bi, ar * bi + ai * br
                result.append(acc[2 * s] + weight * (pr * cr + pi * ci))
                result.append(acc[2 * s + 1] + weight * (pi * cr - pr * ci))
            return tuple(result)

        acc = lax.fori_loop(0, Q, term, tuple(jnp.zeros((8, LANES), f32) for _ in range(8)), unroll=8)
        for s in range(4):
            for part in range(2):
                spread[s, j, part * 8 : part * 8 + 8, :] = acc[2 * s + part] * (unit * unit * unit)
        return carry

    def tiles(start, stop):
        lax.fori_loop(start, stop, tile, 0)

    def store_piece(a, value):
        half_sig[pl.ds(a, 64, stride=4), :] = value

    def collect(p, share):
        for s in range(4):
            for jj in range(4):
                for part in range(2):
                    wide[s, pl.ds(part * 32 + jj, 8, stride=4), :] = spread[s, p * 4 + jj, part * 8 : part * 8 + 8, :]
        regroup(64, lambda s: wide[s], store_piece)
        if share:
            sigma_out[p * HALF : (p + 1) * HALF] = half_sig[...].astype(bf16)
        for n in range(16):
            sig[n * N + p * 16 : n * N + p * 16 + 16] = half_sig[n * 16 : n * 16 + 16]

    return tiles, collect


ENERGY_SCRATCH = [
    pltpu.VMEM((4, 64, LANES), i32),
    pltpu.VMEM((TILES, 4, 8, LANES), i32),
    pltpu.VMEM((4, TILES, 16, LANES), f32),
    pltpu.VMEM((4, 64, LANES), f32),
    pltpu.VMEM((HALF, LANES), f32),
    pltpu.VMEM((WIDE, LANES), f32),
]


def final_kernel(
    rows_first, sigma_first, held, pair_wide, weight_wide, rows_ref, sigma_ref,
    field, packed, spread, wide, half_sig, sig, rows_out, sigma_out, sems,
):
    copies = [
        pltpu.make_async_copy(rows_first, rows_ref.at[0, 0], sems.at[0]),
        pltpu.make_async_copy(sigma_first, sigma_ref.at[0, 0], sems.at[1]),
        pltpu.make_async_copy(rows_out, rows_ref.at[1, 0], sems.at[2]),
        pltpu.make_async_copy(sigma_out, sigma_ref.at[1, 0], sems.at[3]),
    ]
    copies[0].start()
    copies[1].start()
    rows_out[...] = held[...].T
    copies[2].start()
    tiles, collect = self_energy(held, None, pair_wide, weight_wide, field, packed, spread, wide, half_sig, sig)
    tiles(0, 8)
    collect(0, False)
    collect(1, False)
    sigma_out[...] = sig[...].T.astype(bf16)
    copies[3].start()
    for copy in copies:
        copy.wait()


def window_kernel(
    green_hbm, panel_hbm, inv_in, pair_wide, weight_wide,
    rows_ref, sigma_ref, last_ref,
    field, packed, spread, wide, half_sig, sig,
    green, panel_raw, panel_now, panel_next, inv_ref, held, sigma_out,
    sib_send, sib_recv, sums, msg_send, msg_recv, unit_send, unit_recv,
    load_sem, in_sem, inv_ss, inv_rs, sib_ss, sib_rs, msg_ss, msg_rs, unit_ss, unit_rs,
    st_ss, st_rs, st_ls, a1_ss, a1_rs, a2_ss, a2_rs, b1_ss, b1_rs, b2_ss, b2_rs,
):
    hist, tsec = lax.axis_index("hist"), lax.axis_index("tsec")
    chip, core = hist // 2, hist % 2
    z, y = tsec // 4, tsec % 4
    sibling = chip * 2 + 1 - core
    holder = core == y // 2
    depth = panel_now.shape[1]

    def at_chip(o, which):
        return ((chip + o) % 4) * 2 + which

    def loads(d):
        lanes = pl.ds(pl.multiple_of(d * LANES, LANES), LANES)
        return [
            pltpu.make_async_copy(
                green_hbm.at[part, :, lanes],
                green.at[d, :, pl.ds(part * LANES, LANES)],
                load_sem.at[d, part],
            )
            for part in range(2)
        ]

    panel_load = pltpu.make_async_copy(panel_hbm, panel_raw, in_sem.at[0])
    inv_keep = pltpu.make_async_copy(inv_in, inv_ref.at[core], in_sem.at[1])
    panel_load.start()
    for o in (2, 1, 3, 0):
        for d in (at_chip(o, 1 - core), at_chip(o, core)):
            for copy in loads(d):
                copy.start()
    inv_keep.start()

    barrier = pltpu.get_barrier_semaphore()

    def greet(h, t):
        pl.semaphore_signal(barrier, inc=1, device_id={"hist": h, "tsec": t}, device_id_type=MESH)

    greet(sibling, tsec)
    for o in range(1, 4):
        greet(at_chip(o, core), tsec)
        greet(hist, z * 4 + (y + o) % 4)
        greet(hist, ((z + o) % 4) * 4 + y)
    for h in range(8):
        @pl.when(jnp.logical_and(holder, jnp.logical_or(hist != h, z != chip)))
        def _():
            greet(h, chip * 4 + y)

    panel_load.wait()
    for r in range(depth // HALF):
        panel_now[:, r * HALF : (r + 1) * HALF] = panel_raw[r * HALF : (r + 1) * HALF, :].T
    own_part = hist == 2 * z + y // 2
    is_last = jnp.where(hist == 7, 1.0, 0.0).astype(f32)

    def remote(src, dst, ss, rs, h, t):
        return pltpu.make_async_remote_copy(
            src_ref=src, dst_ref=dst, send_sem=ss, recv_sem=rs,
            device_id={"hist": h, "tsec": t}, device_id_type=MESH,
        )

    inv_give = remote(inv_in, inv_ref.at[core], inv_ss, inv_rs, sibling, tsec)
    inv_take = remote(inv_in, inv_ref.at[1 - core], inv_ss, inv_rs, sibling, tsec)

    def memory(run):
        k = min(run, 1)
        count = WIDE if run == 0 else HALF
        half = count // 2
        base = HALF if run == 2 else 0
        upper, lower = pl.ds(base, half), pl.ds(base + half, half)
        whole, msg_rows = pl.ds(base, count), pl.ds(base // 2, half)

        def chunk(d):
            left = panel_now[...] if run == 0 else panel_next[base : base + count, :]
            out = dot(left, green[d])
            re = out[:half, :LANES] - out[half:, LANES:]
            im = out[half:, :LANES] + out[:half, LANES:]
            if k == 0:
                tail = green[d, green.shape[1] - HALF :, :].astype(f32) * is_last
                re, im = re + tail[:, :LANES], im + tail[:, LANES:]
            return re, im

        def swap(i):
            return remote(
                sib_send.at[k, i, whole], sib_recv.at[k, i, whole], sib_ss.at[run, i], sib_rs.at[run, i], sibling, tsec
            )

        def messages(o):
            there, n = at_chip(o, core), o - 1
            return (
                remote(msg_send.at[k, n, msg_rows], msg_recv.at[k, n, msg_rows], msg_ss.at[run, n], msg_rs.at[run, n], there, tsec),
                remote(unit_send.at[run, n], unit_recv.at[run, n], unit_ss.at[run, n], unit_rs.at[run, n], there, tsec),
            )

        def offset(i):
            return jnp.where(i == 0, 2, jnp.where(i == 1, 1, jnp.where(i == 2, 3, 0)))

        def finish(last):
            swap(last).wait()
            o = offset(last)
            re = sums[k, last, upper] + sib_recv[k, last, upper]
            im = sums[k, last, lower] + sib_recv[k, last, lower]
            peak = jnp.maximum(jnp.max(jnp.maximum(jnp.abs(re), jnp.abs(im))), 1e-30)
            scale = PEAK / peak
            high = jnp.round(re * scale).astype(i32)
            low = jnp.round(im * scale).astype(i32)
            msg_send[k, o - 1, msg_rows] = lax.shift_left(high, 16) | (low & 0xFFFF)
            unit_send[run, o - 1] = jnp.full((8, LANES), 1.0, f32) * (peak / PEAK)
            for copy in messages(o):
                copy.start()

        late = 0

        def step(i, carry):
            far = at_chip(offset(i), 1 - core)
            if k == 0:
                for copy in loads(far):
                    copy.wait()
            re, im = chunk(far)
            sib_send[k, i, upper] = re
            sib_send[k, i, lower] = im
            if k == 0:
                @pl.when(i == 0)
                def _():
                    pl.semaphore_wait(barrier, jnp.where(own_part, 13, 14))

                swap(i).start()

                @pl.when(i == 3)
                def _():
                    inv_give.start()
            else:
                swap(i).start()

            @pl.when(i > late)
            def _():
                finish(i - 1 - late)

            near = at_chip(offset(i), core)
            if k == 0:
                for copy in loads(near):
                    copy.wait()
            re, im = chunk(near)
            sums[k, i, upper] = re
            sums[k, i, lower] = im
            return carry

        lax.fori_loop(0, 4, step, 0)
        for last in range(3 - late, 3):
            finish(last)
        swap(3).wait()

        def collect():
            re = sums[k, 3, upper] + sib_recv[k, 3, upper]
            im = sums[k, 3, lower] + sib_recv[k, 3, lower]
            for o in (1, 3, 2):
                for copy in messages(o):
                    copy.wait()
                both = msg_recv[k, o - 1, msg_rows]
                unit = unit_recv[run, o - 1, :1, :1]
                re = re + lax.shift_right_arithmetic(both, 16).astype(f32) * unit
                im = im + lax.shift_right_arithmetic(lax.shift_left(both, 16), 16).astype(f32) * unit
            return re, im

        return collect

    def first(p, j):
        slot = pl.ds(pl.multiple_of((y % 2) * 1024 + hist * LANES, LANES), LANES)
        rows = pl.ds(p * HALF + j * 64, 64)
        return remote(
            sigma_out.at[rows], panel_next.at[rows, slot], st_ss.at[p, j], st_rs.at[p, hist], 2 * z + y // 2, 4 * j + y
        )

    def first_here(p, j):
        slot = pl.ds(pl.multiple_of((y % 2) * 1024 + hist * LANES, LANES), LANES)
        rows = pl.ds(p * HALF + j * 64, 64)
        return pltpu.make_async_copy(sigma_out.at[rows], panel_next.at[rows, slot], st_ls.at[p])

    def piece(p, second, j, odd):
        rows = pl.ds(pl.multiple_of(p * HALF + j * 64 + second * 32, 32), 32)
        return panel_next.at[rows, pl.ds(pl.multiple_of(odd * 1024, 1024), 1024)]

    def pass_on(p, second, j, odd, ss, rs, t):
        return remote(piece(p, second, j, odd), piece(p, second, j, odd), ss, rs, hist, t)

    def along_y(n):
        return z * 4 + (y + n) % 4

    def along_z(n):
        return ((z + n) % 4) * 4 + y

    def a1(p, n):
        return pass_on(p, 0, z, y % 2, a1_ss.at[p, n - 1], a1_rs.at[p, y % 2], along_y(n))

    def b1(p, n):
        return pass_on(p, 1, z, y % 2, b1_ss.at[p, n - 1], b1_rs.at[p, z], along_z(n))

    def a2(p, odd, n):
        return pass_on(p, 0, z, odd, a2_ss.at[p, odd, n - 1], a2_rs.at[p, z, odd], along_z(n))

    def b2(p, m, n):
        j = (z + m) % 4
        return pass_on(p, 1, j, y % 2, b2_ss.at[p, m, n - 1], b2_rs.at[p, j, y % 2], along_y(n))

    def exchange(p):
        for j in range(4):
            here = jnp.logical_and(own_part, z == j)

            @pl.when(jnp.logical_not(here))
            def _():
                first(p, j).start()

            @pl.when(here)
            def _():
                first_here(p, j).start()

    def arrived(p, second, j, odd, rs):
        pass_on(p, second, j, odd, a1_ss.at[p, 0], rs, along_y(1)).wait_recv()

    def relay_first(p):
        @pl.when(holder)
        def _():
            for h in range(8):
                slot = pl.ds(pl.multiple_of((y % 2) * 1024 + h * LANES, LANES), LANES)
                rows = pl.ds(pl.multiple_of(p * HALF + z * 64, 64), 64)

                @pl.when(jnp.logical_or(hist != h, z != chip))
                def _():
                    remote(
                        sigma_out.at[pl.ds(0, 64)], panel_next.at[rows, slot], st_ss.at[p, 0], st_rs.at[p, h], sibling, tsec
                    ).wait_recv()

            for j in range(4):
                @pl.when(jnp.logical_and(own_part, z == j))
                def _():
                    first_here(p, j).wait()

            for n in (2, 1, 3):
                a1(p, n).start()
                b1(p, n).start()
            for n in (2, 1, 3):
                a2(p, y % 2, n).start()
                b2(p, 0, n).start()

    def relay_second(p):
        for odd in range(2):
            @pl.when(2 * core + odd != y)
            def _():
                arrived(p, 0, z, odd, a1_rs.at[p, odd])
                for n in (2, 1, 3):
                    a2(p, odd, n).start()

        @pl.when(holder)
        def _():
            for m in (1, 3, 2):
                j = (z + m) % 4
                arrived(p, 1, j, y % 2, b1_rs.at[p, j])
                for n in (2, 1, 3):
                    b2(p, m, n).start()

    def settle(p):
        for odd in range(2):
            for m in (1, 3, 2):
                j = (z + m) % 4
                arrived(p, 0, j, odd, a2_rs.at[p, j, odd])

            @pl.when(2 * core + odd != y)
            def _():
                for j in range(4):
                    arrived(p, 1, j, odd, b2_rs.at[p, j, odd])

    def drain(p):
        for j in range(4):
            @pl.when(jnp.logical_not(jnp.logical_and(own_part, z == j)))
            def _():
                first(p, j).wait_send()
        for n in range(1, 4):
            for odd in range(2):
                a2(p, odd, n).wait_send()

        @pl.when(holder)
        def _():
            for n in range(1, 4):
                a1(p, n).wait_send()
                b1(p, n).wait_send()
                for m in range(4):
                    b2(p, m, n).wait_send()

    def solve(k, rhs):
        both = jnp.concatenate([rhs[:HALF], rhs[HALF:]], axis=1)
        high = both.astype(bf16)
        low = (both - high.astype(f32)).astype(bf16)
        out = dot(inv_ref[k], high)
        out = out[:WIDE] + out[WIDE:] + dot(inv_ref[k, :WIDE], low)
        held[:HALF] = out[:HALF, :LANES] - out[HALF:, LANES:]
        held[HALF:] = out[HALF:, :LANES] + out[:HALF, LANES:]

    re, im = memory(0)()
    inv_keep.wait()
    inv_take.wait_recv()
    solve(0, jnp.concatenate([re, im], axis=0))
    tiles, collect = self_energy(
        held, sigma_out, pair_wide, weight_wide, field, packed, spread, wide, half_sig, sig
    )
    tiles(0, 4)
    collect(0, True)
    exchange(0)
    tiles(4, 8)
    collect(1, True)
    exchange(1)
    relay_first(0)
    relay_second(0)
    rows_ref[...] = held[...].T
    sigma_ref[...] = sig[...].T.astype(bf16)
    relay_first(1)
    relay_second(1)
    settle(0)
    results = [memory(1)]
    settle(1)
    results.append(memory(2))
    for p in range(2):
        re, im = results[p]()
        for n in range(8):
            for part, value in enumerate((re, im)):
                at = part * HALF + n * N + p * 16
                held[at : at + 16] = held[at : at + 16] + value[n * 16 : n * 16 + 16]
    solve(1, held[...])
    last_ref[...] = held[...]
    inv_give.wait_send()
    for p in range(2):
        drain(p)


def per_device(hist_green, sigma_panel, step_operator, coupling, pair_index):
    inverse, pairs, weights = prepare(step_operator, pair_index.reshape(3 * Q, PAIRS), coupling)
    depth = sigma_panel.shape[0]
    anywhere = pl.BlockSpec(memory_space=pl.ANY)
    vmem = pl.BlockSpec(memory_space=pltpu.VMEM)
    dma = pltpu.SemaphoreType.DMA
    rows_first, sigma_first, last = pl.pallas_call(
        window_kernel,
        out_shape=(
            jax.ShapeDtypeStruct((LANES, WIDE), f32),
            jax.ShapeDtypeStruct((LANES, WIDE), bf16),
            jax.ShapeDtypeStruct((WIDE, LANES), f32),
        ),
        in_specs=[anywhere, anywhere, vmem, vmem, vmem],
        out_specs=(vmem, vmem, vmem),
        scratch_shapes=ENERGY_SCRATCH + [
            pltpu.VMEM((8, depth, 2 * LANES), bf16),
            pltpu.VMEM((depth, WIDE), bf16),
            pltpu.VMEM((WIDE, depth), bf16),
            pltpu.VMEM((WIDE, depth), bf16),
            pltpu.VMEM((NBLK, 2 * WIDE, HALF), bf16),
            pltpu.VMEM((WIDE, LANES), f32),
            pltpu.VMEM((WIDE, LANES), bf16),
            pltpu.VMEM((NBLK, 4, WIDE, LANES), f32),
            pltpu.VMEM((NBLK, 4, WIDE, LANES), f32),
            pltpu.VMEM((NBLK, 4, WIDE, LANES), f32),
            pltpu.VMEM((NBLK, 3, HALF, LANES), i32),
            pltpu.VMEM((NBLK, 3, HALF, LANES), i32),
            pltpu.VMEM((3, 3, 8, LANES), f32),
            pltpu.VMEM((3, 3, 8, LANES), f32),
            dma((8, 2)), dma((2,)), dma(()), dma(()),
            dma((3, 4)), dma((3, 4)),
            dma((3, 3)), dma((3, 3)),
            dma((3, 3)), dma((3, 3)),
            dma((2, 4)), dma((2, 8)), dma((2,)),
            dma((2, 3)), dma((2, 2)), dma((2, 2, 3)), dma((2, 4, 2)),
            dma((2, 3)), dma((2, 4)), dma((2, 4, 3)), dma((2, 4, 2)),
        ],
        compiler_params=pltpu.CompilerParams(
            collective_id=0, has_side_effects=True, vmem_limit_bytes=50 << 20
        ),
    )(hist_green, sigma_panel, inverse, pairs, weights)
    return pl.pallas_call(
        final_kernel,
        out_shape=(
            jax.ShapeDtypeStruct((NBLK, 1, LANES, WIDE), f32),
            jax.ShapeDtypeStruct((NBLK, 1, LANES, WIDE), bf16),
        ),
        in_specs=[anywhere, anywhere, vmem, vmem, vmem],
        out_specs=(anywhere, anywhere),
        scratch_shapes=ENERGY_SCRATCH + [
            pltpu.VMEM((LANES, WIDE), f32),
            pltpu.VMEM((LANES, WIDE), bf16),
            dma((4,)),
        ],
        compiler_params=pltpu.CompilerParams(vmem_limit_bytes=24 << 20),
    )(rows_first, sigma_first, last, pairs, weights)


def solution(mesh):
    return jax.shard_map(
        per_device,
        mesh=mesh,
        in_specs=(P(None, "hist", "tsec"), P("hist", None), P(), P(), P()),
        out_specs=(P(None, "tsec", "hist", None), P(None, "tsec", "hist", None)),
        check_vma=False,
    )
```
